256 devices in a mesh: leaf: 64 (over x, z, core), rhs: 4 (over y).
Axes of the slice: x: 4, y: 4, z: 8, core: 2. Of those that a mesh axis runs over, the one named last changes fastest.
Arguments:
- fields: bfloat16 [131072, 1024], P('leaf', 'rhs'), may hold values from -6 to 6
- owner: int32 [131072, 1], P('leaf'), may hold values from 0 to 63; in each aligned block of 2048 rows (0 to 2047, 2048 to 4095, ...) at most 64 rows name the same one
- source_basis: bfloat16 [131072, 256], P('leaf'), may hold values from -0.125 to 0.125
- field_basis: bfloat16 [131072, 256], P('leaf'), may hold values from -0.375 to 0.375
- transfer: bfloat16 [64, 3, 256, 512], P('leaf', None, 'rhs'), may hold values from -0.25 to 0.25
- near_blocks: bfloat16 [512, 7, 256, 256], P('leaf'), may hold values from -0.25 to 0.25
- near_index: int32 [512, 7], P('leaf'), may hold values from 0 to 7
- near_count: int32 [512], P('leaf'), may hold values from 1 to 7
Outputs:
- scattered: bfloat16 [131072, 1024], P('leaf', 'rhs')
The draws below stay inside these ranges and needn't reach their ends.
Inputs may be any that keep to these rules, and one draw needn't show every extreme that they name: In the rows of one group of 2048 rows at most 64 name one owner; in some group one owner is named by exactly 64. `near_index`: Row-block numbers counted within the same group of 8 row blocks.
All inputs are finite; a program needn't handle non-finite values.
Results may differ from the reference program's by a relative error of at most 0.006.
Values may be sent and summed in bfloat16 or wider, within the bound.
A program may use at most 128 MiB of HBM per device.

```python
import math
import jax
import jax.numpy as jnp
import numpy as np
from jax import lax

K = 256
LEVELS = 3
BLK = 256
NEAR = 7
ROWS_DEV = 2048
COLS = 1024
ROWS = 131072
CAP = 64
BPD = 8
BLOCKS = 512
N_LEAF = 64


def draw_near_count(key, part):
    counts = jax.random.randint(key, (BLOCKS,), 1, NEAR + 1, dtype=jnp.int32)
    chosen_spots = jax.random.randint(jax.random.fold_in(key, 11), (2,), 0, BLOCKS, dtype=jnp.int32)
    second_spot = (chosen_spots[0] + 1 + chosen_spots[1] % (BLOCKS - 1)) % BLOCKS
    places = jnp.arange(BLOCKS, dtype=jnp.int32)
    counts = jnp.where(places == chosen_spots[0], NEAR, counts)
    counts = jnp.where(places == second_spot, 1, counts)
    return counts.astype(jnp.int32)


def touch_ends(array, rng, least, largest):
    spot = [jax.random.randint(jax.random.fold_in(rng, axis), (), 0, length) for axis, length in enumerate(array.shape)]
    widest = array.shape.index(max(array.shape))
    neighbour = spot[:widest] + [(spot[widest] + 1) % array.shape[widest]] + spot[widest + 1:]
    return array.at[tuple(spot)].set(least).at[tuple(neighbour)].set(largest)


def levels(own_key, dims, split, smallest, largest):
    def one(dim, parts):
        steps = jax.random.uniform(jax.random.fold_in(jax.random.fold_in(own_key, 6), dim), (parts,), jnp.float32, smallest / len(split), largest / len(split))
        return jnp.repeat(jnp.exp(steps), dims[dim] // parts).reshape((-1,) + (1,) * (len(dims) - dim - 1))

    level = one(*split[0])
    for cut in split[1:]:
        level = level * one(*cut)
    return level


def shared_out(own_key, own, number, rows, number_of, top, reach, skew):
    order = jax.random.permutation(own_key, number_of)
    crowded, ordinary = shares(number_of, rows * top, reach, skew, True), shares(number_of, rows * top, reach, skew, False)
    places = jnp.arange(number_of)

    def named(sizes, offset_by):
        used = int((sizes > 0).sum())
        fixed = max(1, used // 4)
        shifted = fixed + (places - fixed + offset_by * (used - fixed)) % max(1, number_of - fixed)
        return jnp.zeros((number_of,), jnp.int32).at[order[jnp.where(places < fixed, places, shifted)]].set(jnp.asarray(sizes, jnp.int32))

    sizes = jnp.where(number % 4 == 0, named(crowded, number // 4), named(ordinary, number - number // 4 - 1))
    mixed = jax.random.permutation(jax.random.fold_in(own, 3), number_of)
    donor, receiver = mixed[0:number_of // 2 * 2:2], mixed[1:number_of // 2 * 2:2]
    room = jnp.minimum(sizes[donor] - 1, reach - sizes[receiver]) // 2
    room = jnp.where((donor == order[0]) | (receiver == order[0]) | (sizes[receiver] == 0), 0, jnp.maximum(room, 0))
    shifted = jax.random.randint(jax.random.fold_in(own, 4), (number_of // 2,), 0, 1 << 20) % (room + 1)
    sizes = sizes.at[donor].add(-shifted).at[receiver].add(shifted)
    labels = jnp.searchsorted(jnp.cumsum(sizes), jnp.arange(rows * top), side="right").astype(jnp.int32)
    table = labels.reshape(top, rows).T
    table = table[jax.random.permutation(jax.random.fold_in(own, 1), rows)]
    offset_by = jax.random.randint(jax.random.fold_in(own, 2), (rows, 1), 0, top)
    return jnp.take_along_axis(table, (jnp.arange(top)[None, :] + offset_by) % top, axis=1)


def shares(count, total, bound, lean, full):
    loads = [(1 << 20) // math.isqrt(standing ** lean) + 1 for standing in range(1, count + 1)]
    largest = bound if full else min(bound, max(-(-total // count), total * loads[0] // sum(loads)))
    least = 1 if total - largest >= count - 1 else 0
    given, surplus = [largest] + [least] * (count - 1), total - largest - least * (count - 1)
    while surplus > 0:
        movable = [i for i in range(1, count) if given[i] < largest] or [i for i in range(1, count) if given[i] < bound]
        pool, remaining = sum([loads[i] for i in movable]), surplus
        for i in movable:
            extra = min(bound - given[i], max(1, remaining * loads[i] // pool), surplus)
            given[i] = given[i] + extra
            surplus = surplus - extra
    return np.array(given)


def scatter_about(rng, extent, width, bound, pieces=(), kind=jnp.bfloat16):
    values = jax.random.normal(rng, extent, jnp.float32) * width
    if len(pieces) > 0:
        values = levels(rng, extent, pieces, -0.22, 0.18) * values
    return jnp.clip(values, min=-bound, max=bound).astype(kind)


def setup_inputs(seed: int = 0) -> dict:
    keys = jax.random.split(jax.random.key(seed), 9)
    fields = scatter_about(keys[0], (ROWS, COLS), 1.0, 6.0, ((0, 64), (1, 4)))
    owner_keys = jax.random.split(jax.random.fold_in(keys[1], 1), ROWS // ROWS_DEV)
    owner_turns = jax.random.permutation(jax.random.fold_in(keys[1], 3), ROWS // ROWS_DEV)
    owner = jax.vmap(lambda own, number: shared_out(jax.random.fold_in(keys[1], 2), own, number, ROWS_DEV, N_LEAF, 1, CAP, 2))(owner_keys, owner_turns).reshape((ROWS, 1))
    source_basis = scatter_about(keys[2], (ROWS, K), ROWS_DEV ** -0.5, 0.125, ((0, 64),))
    field_basis = scatter_about(keys[3], (ROWS, K), K ** -0.5, 0.375, ((0, 64),))
    transfer = scatter_about(keys[4], (N_LEAF, LEVELS, K, 2 * K), (2 * K) ** -0.5, 0.25, ((0, 64), (2, 4)))
    near_blocks = scatter_about(keys[5], (BLOCKS, NEAR, BLK, BLK), (2 * BLK) ** -0.5, 0.25, ((0, 64),))
    near_index = touch_ends(jax.random.randint(keys[6], (BLOCKS, NEAR), 0, BPD), jax.random.fold_in(keys[6], 1), 0, BPD - 1).astype(jnp.int32)
    near_count = draw_near_count(jax.random.fold_in(keys[8], 71), 0)
    return dict(fields=fields, owner=owner, source_basis=source_basis, field_basis=field_basis, transfer=transfer, near_blocks=near_blocks, near_index=near_index, near_count=near_count)


def slot_numbers(owners_of):
    onehot = (owners_of[:, None] == jnp.arange(N_LEAF, dtype=jnp.int32)[None, :]).astype(jnp.int32)
    before = jnp.cumsum(onehot, axis=0) - onehot
    rank_in = jnp.sum(before * onehot, axis=1)
    return (owners_of * CAP + rank_in).astype(jnp.int32)


def reference(fields, owner, source_basis, field_basis, transfer, near_blocks, near_index, near_count):
    col_count = fields.shape[1]
    x_groups = fields.reshape(N_LEAF, ROWS_DEV, col_count)
    owner_groups = owner[:, 0].reshape(N_LEAF, ROWS_DEV)
    source_groups = source_basis.reshape(N_LEAF, ROWS_DEV, K)
    field_groups = field_basis.reshape(N_LEAF, ROWS_DEV, K)

    def add_source(totals, inputs):
        x_one, owner_one, source_one = inputs
        slot_index = slot_numbers(owner_one)
        x_slots = jnp.zeros((N_LEAF * CAP, col_count), jnp.float32).at[slot_index].set(x_one.astype(jnp.float32))
        v_slots = jnp.zeros((N_LEAF * CAP, K), jnp.float32).at[slot_index].set(source_one.astype(jnp.float32))
        terms = jnp.einsum('bck,bcn->bkn', v_slots.reshape(N_LEAF, CAP, K), x_slots.reshape(N_LEAF, CAP, col_count))
        return totals + terms, None

    totals, _ = lax.scan(add_source, jnp.zeros((N_LEAF, K, col_count), jnp.float32), (x_groups, owner_groups, source_groups))
    coefficients = totals.astype(jnp.bfloat16)
    for level_num in range(LEVELS):
        stride = 2 ** level_num
        paired = coefficients.reshape(N_LEAF // (2 * stride), 2, stride, K, col_count)[:, ::-1].reshape(N_LEAF, K, col_count)
        stacked = jnp.concatenate([coefficients, paired], axis=1).astype(jnp.float32)
        coefficients = jnp.einsum('bij,bjn->bin', transfer[:, level_num].astype(jnp.float32), stacked).astype(jnp.bfloat16)
    final_coeffs = coefficients.astype(jnp.float32)

    index_groups = near_index.reshape(N_LEAF, BPD, NEAR)
    count_groups = near_count.reshape(N_LEAF, BPD)
    block_groups = near_blocks.reshape(N_LEAF, BPD, NEAR, BLK, BLK)

    def one_device(inputs):
        x_one, owner_one, field_one, block_weights, index_one, count_one = inputs
        slot_index = slot_numbers(owner_one)
        u_slots = jnp.zeros((N_LEAF * CAP, K), jnp.float32).at[slot_index].set(field_one.astype(jnp.float32))
        far_slots = jnp.einsum('bck,bkn->bcn', u_slots.reshape(N_LEAF, CAP, K), final_coeffs).astype(jnp.bfloat16)
        far_term = far_slots.reshape(N_LEAF * CAP, col_count)[slot_index]
        x_blocks = x_one.reshape(BPD, BLK, col_count)
        chosen = x_blocks[index_one].astype(jnp.float32)
        keep_mask = (jnp.arange(NEAR, dtype=jnp.int32)[None, :] < count_one[:, None]).astype(jnp.float32)
        weighted = block_weights.astype(jnp.float32) * keep_mask[:, :, None, None]
        near_term = jnp.einsum('gjab,gjbn->gan', weighted, chosen).reshape(ROWS_DEV, col_count)
        return (far_term.astype(jnp.float32) + near_term).astype(jnp.bfloat16)

    result = lax.map(one_device, (x_groups, owner_groups, field_groups, block_groups, index_groups, count_groups))
    return result.reshape(N_LEAF * ROWS_DEV, col_count)
```

```python
import jax
import jax.numpy as jnp
from jax import lax
from jax.experimental import pallas as pl
from jax.experimental.pallas import tpu as pltpu
from jax.sharding import PartitionSpec as P

MESH = pl.DeviceIdType.MESH
F32 = jnp.float32
BF16 = jnp.bfloat16
CAP = 64
NX, NZ, NC, NY = 4, 8, 2, 4
NB = NX * NZ * NC


def slot_kernel(owner_ref, slot_ref):
    rows = owner_ref.shape[1]
    step = 256
    below = lax.broadcasted_iota(jnp.int32, (step, step), 0)
    above = lax.broadcasted_iota(jnp.int32, (step, step), 1)
    tri = (below < above).astype(F32).astype(BF16)
    carry = jnp.zeros((NB, 1), F32)
    names = lax.broadcasted_iota(jnp.int32, (NB, step), 0)
    for i in range(rows // step):
        own = owner_ref[:, i * step : (i + 1) * step]
        hot = (names == own).astype(F32)
        before = jnp.dot(hot.astype(BF16), tri, preferred_element_type=F32) + carry
        rank = jnp.sum(before * hot, axis=0, keepdims=True)
        slot_ref[:, i * step : (i + 1) * step] = own * CAP + rank.astype(jnp.int32)
        carry = carry + jnp.sum(hot, axis=1, keepdims=True)


def slots_of(owner_row):
    return pl.pallas_call(
        slot_kernel,
        out_shape=jax.ShapeDtypeStruct(owner_row.shape, jnp.int32),
        in_specs=[pl.BlockSpec(memory_space=pltpu.VMEM)],
        out_specs=pl.BlockSpec(memory_space=pltpu.VMEM),
    )(owner_row)


def leaf_id(x, z, c):
    return x * (NZ * NC) + z * NC + c


def far_kernel(
    slot_ref, x_ref, v_ref, u_ref, t_ref, far_ref,
    sx, rx, us, ring, lvl, part, tg, cb,
    xs_sem, xr_sem, rs_sem, rr_sem, bs_sem, br_sem, ts_sem, tr_sem,
    zs_sem, zr_sem, hs_sem, hr_sem, fs_sem, fr_sem, cs_sem, cr_sem,
):
    leaf = lax.axis_index("leaf")
    y = lax.axis_index("rhs")
    x = leaf // (NZ * NC)
    z = (leaf // NC) % NZ
    c = leaf % NC
    d = 1 - 2 * c

    def dev(xx, zz, cc):
        return {"leaf": leaf_id(xx % NX, zz % NZ, cc), "rhs": y}

    def remote(src, dst, ssem, rsem, who):
        return pltpu.make_async_remote_copy(
            src_ref=src, dst_ref=dst, send_sem=ssem, recv_sem=rsem,
            device_id=who, device_id_type=MESH,
        )

    barrier = pltpu.get_barrier_semaphore()
    peers = [dev(x + dx, z, (c + dc) % NC) for dx in range(NX) for dc in range(NC) if dx or dc]
    z4 = (z // 4) * 4
    z2 = z4 + (z - z4 + 2) % 4
    z1 = (z // 2) * 2 + (1 - z % 2)
    peers += [dev(x, z + 1, c), dev(x, z + NZ - 1, c), dev(x, z2, c)]
    peers += [{"leaf": leaf, "rhs": (y + k) % NY} for k in range(1, NY)]
    for who in peers:
        pl.semaphore_signal(barrier, inc=1, device_id=who, device_id_type=MESH)
    pl.semaphore_wait(barrier, len(peers))

    tcopies = [
        remote(t_ref, tg.at[:, y], ts_sem.at[k - 1], tr_sem.at[k - 1], {"leaf": leaf, "rhs": (y + k) % NY})
        for k in range(1, NY)
    ]
    for cp in tcopies:
        cp.start()
    tg[:, y] = t_ref[...]

    ranks = lax.broadcasted_iota(jnp.int32, (CAP, 1), 0)

    def permute(i, carry):
        slots = slot_ref[...]
        hots = []
        for k in range(NX * NC):
            xx, cc = (x + k // NC) % NX, (c + k % NC) % NC
            zz = (z + NZ - (1 - 2 * cc) * (i + 1)) % NZ
            want = ranks + leaf_id(xx, zz, cc) * CAP
            hots.append((slots == want).astype(F32).astype(BF16))
        hot = jnp.concatenate(hots, axis=0)
        xp = jnp.dot(hot, x_ref[...], preferred_element_type=F32).astype(BF16)
        vp = jnp.dot(hot, v_ref[...], preferred_element_type=F32).astype(BF16)
        rx[i, 0, :, 0:256] = xp[0:CAP]
        rx[i, 0, :, 256:512] = vp[0:CAP]
        sx[i, :, :, 0:256] = xp[CAP:].reshape(NX * NC - 1, CAP, 256)
        sx[i, :, :, 256:512] = vp[CAP:].reshape(NX * NC - 1, CAP, 256)
        for k in range(1, NX * NC):
            remote(
                sx.at[i, k - 1], rx.at[i, k], xs_sem.at[i], xr_sem.at[i],
                dev(x + k // NC, z, (c + k % NC) % NC),
            ).start()
        return carry

    lax.fori_loop(0, NZ, permute, 0)

    def permute_u(i, carry):
        want = lax.broadcasted_iota(jnp.int32, (8 * CAP, 1), 0) + i * (8 * CAP)
        hot = (slot_ref[...] == want).astype(F32).astype(BF16)
        up = jnp.dot(hot, u_ref[...], preferred_element_type=F32).astype(BF16)
        us[pl.ds(i * 8, 8)] = up.reshape(8, CAP, 256)
        return carry

    lax.fori_loop(0, NB // 8, permute_u, 0)

    def product(i):
        pltpu.make_async_copy(rx.at[i, pl.ds(1, 7)], rx.at[i, pl.ds(1, 7)], xr_sem.at[i]).wait()
        vs = rx[i, :, :, 256:512].reshape(NX * NC * CAP, 256)
        xs = rx[i, :, :, 0:256].reshape(NX * NC * CAP, 256)
        return lax.dot_general(vs, xs, (((0,), (0,)), ((), ())), preferred_element_type=F32)

    nxt = dev(x, z + NZ + d, c)

    def ring_copy(s, q):
        return remote(ring.at[s, q], ring.at[s + 1, q], rs_sem.at[s, q], rr_sem.at[s, q], nxt)

    first = product(0)
    for q in range(2):
        ring[0, q] = first[128 * q : 128 * q + 128]
        ring_copy(0, q).start()

    def ring_step(s, carry):
        p = product(s)
        for q in range(2):
            ring_copy(s - 1, q).wait_recv()
            ring[s, q] = ring[s, q] + p[128 * q : 128 * q + 128]
            ring_copy(s, q).start()
        return carry

    lax.fori_loop(1, NZ - 1, ring_step, 0)
    last = product(NZ - 1)
    for q in range(2):
        ring_copy(NZ - 2, q).wait_recv()
        lvl[0, 128 * q : 128 * q + 128, :] = (ring[NZ - 1, q] + last[128 * q : 128 * q + 128]).astype(BF16)

    for cp in tcopies:
        cp.wait_recv()

    mates = [dev(x, z, 1 - c), dev(x, z1, c), dev(x, z2, c)]
    bcopies = []
    for l in range(3):
        cp = remote(lvl.at[l], part.at[l], bs_sem.at[l], br_sem.at[l], mates[l])
        cp.start()
        bcopies.append(cp)
        t = tg[l].reshape(256, 512)
        acc = jnp.dot(t[:, 0:256], lvl[l], preferred_element_type=F32)
        cp.wait_recv()
        acc = acc + jnp.dot(t[:, 256:512], part[l], preferred_element_type=F32)
        if l < 2:
            lvl[l + 1] = acc.astype(BF16)
        else:
            cb[leaf] = acc.astype(BF16)

    waits = []

    def go(cp):
        cp.start()
        waits.append(cp)

    def zsend(sign, j):
        b = leaf_id(x, (z + 2 * NZ - sign * d * (j - 1)) % NZ, c)
        k = j - 1 if sign == 1 else 3 + j
        return remote(cb.at[b], cb.at[b], zs_sem.at[k], zr_sem.at[k], dev(x, z + NZ + sign * d, c))

    order = [0, 1, -1, 2, -2, 3, -3, 4]

    def zpos(n):
        return (z + 2 * NZ - d * order[n]) % NZ

    def have(b, n):
        go(remote(cb.at[b], cb.at[b], cs_sem.at[n], cr_sem.at[n], dev(x, z, 1 - c)))

    def xsend(n, way):
        b = leaf_id(x, zpos(n), c)
        return remote(cb.at[b], cb.at[b], hs_sem.at[n, way], hr_sem.at[n, way], dev(x + (1 if way == 0 else NX - 1), z, c))

    def fsend(n, way):
        b = leaf_id((x + (NX - 1 if way == 0 else 1)) % NX, zpos(n), c)
        half = pl.ds(128 * way, 128)
        return remote(
            cb.at[b, half], cb.at[b, half], fs_sem.at[n, way], fr_sem.at[n, way],
            dev(x + (1 if way == 0 else NX - 1), z, c),
        )

    def xdone(n):
        for way in range(2):
            xsend(n, way).wait_recv()
            go(fsend(n, way))
            have(leaf_id((x + (NX - 1 if way == 0 else 1)) % NX, zpos(n), c), 8 + 2 * n + way)

    def xtwo(n):
        for way in range(2):
            fsend(n, way).wait_recv()
        have(leaf_id((x + 2) % NX, zpos(n), c), 24 + n)

    go(zsend(1, 1))
    go(zsend(-1, 1))
    for n in range(8):
        if n > 0:
            sign, j = (1, order[n]) if order[n] > 0 else (-1, -order[n])
            zsend(sign, j).wait_recv()
            if (sign == 1 and j < 4) or (sign == -1 and j < 3):
                go(zsend(sign, j + 1))
        go(xsend(n, 0))
        go(xsend(n, 1))
        have(leaf_id(x, zpos(n), c), n)
        if n > 1:
            xdone(n - 2)
        if n > 3:
            xtwo(n - 4)
    xdone(6)
    xdone(7)
    for n in range(4, 8):
        xtwo(n)
    for n in range(32):
        remote(cb.at[leaf], cb.at[leaf], cs_sem.at[n], cr_sem.at[n], dev(x, z, 1 - c)).wait_recv()

    def far_one(b, carry):
        far_ref[b] = jnp.dot(us[b], cb[b], preferred_element_type=F32).astype(BF16)
        return carry

    lax.fori_loop(0, NB, far_one, 0)

    for cp in waits:
        cp.wait_send()
    for cp in bcopies:
        cp.wait_send()
    for cp in tcopies:
        cp.wait_send()
    for i in range(NZ):
        pltpu.make_async_copy(sx.at[i], sx.at[i], xs_sem.at[i]).wait()
    for s in range(NZ - 1):
        for q in range(2):
            ring_copy(s, q).wait_send()


def far_slots(slot_row, fields, source_basis, field_basis, transfer):
    vmem = pl.BlockSpec(memory_space=pltpu.VMEM)
    dma = pltpu.SemaphoreType.DMA
    return pl.pallas_call(
        far_kernel,
        out_shape=jax.ShapeDtypeStruct((NB, CAP, 256), BF16),
        in_specs=[vmem] * 5,
        out_specs=vmem,
        scratch_shapes=[
            pltpu.VMEM((NZ, 7, CAP, 512), BF16),
            pltpu.VMEM((NZ, 8, CAP, 512), BF16),
            pltpu.VMEM((NB, CAP, 256), BF16),
            pltpu.VMEM((NZ, 2, 128, 256), F32),
            pltpu.VMEM((3, 256, 256), BF16),
            pltpu.VMEM((3, 256, 256), BF16),
            pltpu.VMEM((3, NY, 64, 512), BF16),
            pltpu.VMEM((NB, 256, 256), BF16),
            dma((NZ,)), dma((NZ,)),
            dma((NZ, 2)), dma((NZ, 2)),
            dma((3,)), dma((3,)),
            dma((3,)), dma((3,)),
            dma((8,)), dma((8,)),
            dma((8, 2)), dma((8, 2)),
            dma((8, 2)), dma((8, 2)),
            dma((32,)), dma((32,)),
        ],
        compiler_params=pltpu.CompilerParams(
            collective_id=0, has_side_effects=True, vmem_limit_bytes=60 * 1024 * 1024
        ),
    )(slot_row, fields, source_basis, field_basis, transfer)


def out_kernel(index_ref, count_ref, blocks_ref, fields_ref, slot_ref, far_ref, out_ref):
    g = pl.program_id(0)
    slots = slot_ref[...]
    acc = None
    for i in range(4):
        want = lax.broadcasted_iota(jnp.int32, (1, 1024), 1) + i * 1024
        hot = (slots == want).astype(F32).astype(BF16)
        piece = jnp.dot(hot, far_ref[i * 1024 : (i + 1) * 1024, :], preferred_element_type=F32)
        acc = piece if acc is None else acc + piece

    def near(j, total):
        src = pl.multiple_of(index_ref[g * 7 + j] * 256, 256)
        return total + jnp.dot(blocks_ref[0, j], fields_ref[pl.ds(src, 256), :], preferred_element_type=F32)

    acc = acc + lax.fori_loop(0, count_ref[g], near, jnp.zeros((256, 256), F32))
    out_ref[...] = acc.astype(BF16)


def combine(near_index, near_count, near_blocks, fields, slot_col, far):
    return pl.pallas_call(
        out_kernel,
        out_shape=jax.ShapeDtypeStruct((2048, 256), BF16),
        grid_spec=pltpu.PrefetchScalarGridSpec(
            num_scalar_prefetch=2,
            grid=(8,),
            in_specs=[
                pl.BlockSpec((1, 7, 256, 256), lambda g, a, b: (g, 0, 0, 0)),
                pl.BlockSpec((2048, 256), lambda g, a, b: (0, 0)),
                pl.BlockSpec((256, 1), lambda g, a, b: (g, 0)),
                pl.BlockSpec((4096, 256), lambda g, a, b: (0, 0)),
            ],
            out_specs=pl.BlockSpec((256, 256), lambda g, a, b: (g, 0)),
        ),
    )(near_index.reshape(-1), near_count, near_blocks, fields, slot_col, far)


def on_device(
    fields, owner, source_basis, field_basis, transfer, near_blocks, near_index, near_count
):
    slot_row = slots_of(owner.reshape(1, -1))
    far = far_slots(slot_row, fields, source_basis, field_basis, transfer[0])
    return combine(
        near_index, near_count, near_blocks, fields, slot_row.reshape(-1, 1), far.reshape(NB * CAP, 256)
    )


def solution(mesh):
    in_specs = (
        P("leaf", "rhs"),
        P("leaf", None),
        P("leaf", None),
        P("leaf", None),
        P("leaf", None, "rhs", None),
        P("leaf", None, None, None),
        P("leaf", None),
        P("leaf"),
    )
    return jax.shard_map(
        on_device, mesh=mesh, in_specs=in_specs, out_specs=P("leaf", "rhs"), check_vma=False
    )
```

```python
import jax
import jax.numpy as jnp
from jax import lax
from jax.experimental import pallas as pl
from jax.experimental.pallas import tpu as pltpu
from jax.sharding import PartitionSpec as P

MESH = pl.DeviceIdType.MESH
F32 = jnp.float32
BF16 = jnp.bfloat16
CAP = 64
NX, NZ, NC, NY = 4, 8, 2, 4
NB = NX * NZ * NC
NG = NX * NC
Q = CAP // NY
ROWS = 2048
HALF = 128
ES = [0, 1, -1, 2, -2, 3, -3, 4]
DIST = [0, 1, 1, 2]
SHIFT = [0, NX - 1, 1, 2]
ROUNDS = [[(e, f) for e in ES for f in range(4) if abs(e) + DIST[f] == r] for r in range(7)]
UNITS = [u for r in ROUNDS for u in r]
FILL = [[[0], []], [[1, 2], []], [[3, 4, 5, 6], [7]]]


def leaf_id(x, z, c):
    return x * (NZ * NC) + z * NC + c


def whole_kernel(
    owner_ref, index_ref, count_ref, x_hbm, v_hbm, u_hbm, t_hbm, n_hbm, out_ref,
    xb, vb, ub, nb, slot, scol, sx, sv, rx, rv, us, ring, lvl, part, tg, cb, acc,
    in_sem, n_sem,
    xs_sem, xr_sem, vs_sem, vr_sem, ys_sem, yr_sem, rs_sem, rr_sem, bs_sem, br_sem, ts_sem, tr_sem,
    zs_sem, zr_sem, hs_sem, hr_sem, fs_sem, fr_sem, cs_sem, cr_sem,
):
    leaf = lax.axis_index("leaf")
    y = lax.axis_index("rhs")
    x = leaf // (NZ * NC)
    z = (leaf // NC) % NZ
    c = leaf % NC
    d = 1 - 2 * c

    def dev(xx, zz, cc):
        return {"leaf": leaf_id(xx % NX, zz % NZ, cc), "rhs": y}

    def peer(k):
        return {"leaf": leaf, "rhs": (y + k) % NY}

    def remote(src, dst, ssem, rsem, who):
        return pltpu.make_async_remote_copy(
            src_ref=src, dst_ref=dst, send_sem=ssem, recv_sem=rsem,
            device_id=who, device_id_type=MESH,
        )

    def arrived(ref, sem):
        pltpu.make_async_copy(ref, ref, sem).wait()

    loads = [
        pltpu.make_async_copy(x_hbm, xb, in_sem.at[0]),
        pltpu.make_async_copy(v_hbm, vb, in_sem.at[1]),
        pltpu.make_async_copy(t_hbm, tg.at[:, y], in_sem.at[2]),
        pltpu.make_async_copy(u_hbm, ub, in_sem.at[3]),
    ]
    for cp in loads:
        cp.start()

    barrier = pltpu.get_barrier_semaphore()
    peers = [dev(x + dx, z, (c + dc) % NC) for dx in range(NX) for dc in range(NC) if dx or dc]
    z4 = (z // 4) * 4
    z2 = z4 + (z - z4 + 2) % 4
    z1 = (z // 2) * 2 + (1 - z % 2)
    peers += [dev(x, z + 1, c), dev(x, z + NZ - 1, c), dev(x, z2, c)]
    peers += [peer(k) for k in range(1, NY)]
    for who in peers:
        pl.semaphore_signal(barrier, inc=1, device_id=who, device_id_type=MESH)

    step = 256
    below = lax.broadcasted_iota(jnp.int32, (step, step), 0)
    above = lax.broadcasted_iota(jnp.int32, (step, step), 1)
    tri = (below < above).astype(F32).astype(BF16)
    carry = jnp.zeros((NB, 1), F32)
    names = lax.broadcasted_iota(jnp.int32, (NB, step), 0)
    for i in range(ROWS // step):
        own = owner_ref[:, i * step : (i + 1) * step]
        hot = (names == own).astype(F32)
        before = jnp.dot(hot.astype(BF16), tri, preferred_element_type=F32) + carry
        rank = jnp.sum(before * hot, axis=0, keepdims=True)
        slot[:, i * step : (i + 1) * step] = own.astype(F32) * CAP + rank
        carry = carry + jnp.sum(hot, axis=1, keepdims=True)

    pl.semaphore_wait(barrier, len(peers))
    for cp in loads[:3]:
        cp.wait()
    nloads = [pltpu.make_async_copy(n_hbm.at[g], nb.at[g], n_sem.at[g]) for g in range(8)]
    for cp in nloads:
        cp.start()

    rel = lax.broadcasted_iota(jnp.int32, (CAP, 1), 0)
    ranks = ((y + NY - rel // Q) % NY) * Q + rel % Q

    def permute(i):
        slots = slot[...]
        hots = []
        for k in range(NG):
            xx, cc = (x + k // NC) % NX, (c + k % NC) % NC
            zz = (z + NZ - (1 - 2 * cc) * (i + 1)) % NZ
            want = (ranks + leaf_id(xx, zz, cc) * CAP).astype(F32)
            hots.append((slots == want).astype(F32).astype(BF16))
        xp = jnp.dot(jnp.concatenate(hots, axis=0), xb[...].reshape(ROWS, 256), preferred_element_type=F32).astype(BF16)
        quarter = jnp.concatenate([h[0:Q] for h in hots], axis=0)
        vp = jnp.dot(quarter, vb[...], preferred_element_type=F32).astype(BF16)
        rx[i, :, 0] = xp[0:CAP].reshape(NY, Q, 256)
        rv[i, 0, 0] = vp[0:Q]
        sx[i] = xp[CAP:].reshape(NG - 1, NY, Q, 256)
        sv[i] = vp[Q:].reshape(NG - 1, Q, 256)
        for k in range(1, NG):
            who = dev(x + k // NC, z, (c + k % NC) % NC)
            remote(sv.at[i, k - 1], rv.at[i, 0, k], vs_sem.at[i], vr_sem.at[i], who).start()
        for k in range(1, NG):
            who = dev(x + k // NC, z, (c + k % NC) % NC)
            remote(sx.at[i, k - 1], rx.at[i, :, k], xs_sem.at[i], xr_sem.at[i], who).start()

    def share(i):
        arrived(rv.at[i, 0, pl.ds(1, NG - 1)], vr_sem.at[i])
        for k in range(1, NY):
            remote(rv.at[i, 0], rv.at[i, k], ys_sem.at[i], yr_sem.at[i], peer(k)).start()

    def place(i):
        want = (lax.broadcasted_iota(jnp.int32, (8 * CAP, 1), 0) + i * (8 * CAP)).astype(F32)
        hot = (slot[...] == want).astype(F32).astype(BF16)
        up = jnp.dot(hot, ub[...], preferred_element_type=F32).astype(BF16)
        us[pl.ds(i * 8, 8)] = up.reshape(8, CAP, 256)

    def near(i):
        nloads[i].wait()
        total = jnp.zeros((256, 256), F32)
        for j in range(7):
            keep = jnp.minimum(jnp.maximum(count_ref[i] - j, 0), 1).astype(F32)
            term = jnp.dot(nb[i, j], xb[index_ref[i, j]], preferred_element_type=F32)
            total = total + term * keep
        acc[i * 256 : i * 256 + 256, :] = total

    def product(i):
        arrived(rx.at[i, :, pl.ds(1, NG - 1)], xr_sem.at[i])
        arrived(rv.at[i, pl.ds(1, NY - 1)], yr_sem.at[i])
        vs = rv[i].reshape(NG * CAP, 256)
        xs = rx[i].reshape(NG * CAP, 256)
        return lax.dot_general(vs, xs, (((0,), (0,)), ((), ())), preferred_element_type=F32)

    nxt = dev(x, z + NZ + d, c)

    def ring_copy(s, q):
        return remote(ring.at[s, q], ring.at[s + 1, q], rs_sem.at[s, q], rr_sem.at[s, q], nxt)

    def ring_first():
        p = product(0)
        for q in range(2):
            ring[0, q] = p[:, HALF * q : HALF * q + HALF]
            ring_copy(0, q).start()

    def ring_step(s):
        p = product(s)
        for q in range(2):
            ring_copy(s - 1, q).wait_recv()
            ring[s, q] = ring[s, q] + p[:, HALF * q : HALF * q + HALF]
            ring_copy(s, q).start()

    tcopies = [
        remote(tg.at[:, y], tg.at[:, y], ts_sem.at[k - 1], tr_sem.at[k - 1], peer(k)) for k in range(1, NY)
    ]
    for cp in tcopies:
        cp.start()
    permute(0)
    permute(1)
    loads[3].wait()
    permute(2)
    share(0)
    place(0)
    permute(3)
    share(1)
    ring_first()
    place(1)

    def step_on(i, carry):
        permute(i + 2)
        share(i)
        ring_step(i - 1)
        place(i)
        return carry

    lax.fori_loop(2, NZ - 2, step_on, 0)
    for i in (NZ - 2, NZ - 1):
        share(i)
        ring_step(i - 1)
        place(i)
    for i in range(ROWS // 128):
        row = jnp.broadcast_to(slot[:, i * 128 : (i + 1) * 128], (128, 128))
        scol[i * 128 : (i + 1) * 128, :] = jnp.transpose(row)
    for cp in tcopies:
        cp.wait_recv()

    mates = [dev(x, z, 1 - c), dev(x, z1, c), dev(x, z2, c)]

    def swap(l, q):
        return remote(lvl.at[l, q], part.at[l, q], bs_sem.at[l, q], br_sem.at[l, q], mates[l])

    last = product(NZ - 1)
    for q in range(2):
        ring_copy(NZ - 2, q).wait_recv()
        lvl[0, q] = (ring[NZ - 1, q] + last[:, HALF * q : HALF * q + HALF]).astype(BF16)
        swap(0, q).start()

    sent = []

    def go(cp):
        cp.start()
        sent.append(cp)

    def item(e, f):
        return leaf_id((x + SHIFT[f]) % NX, (z + 2 * NZ - d * e) % NZ, c)

    def zsend(h, e, f, to):
        b = item(e, f)
        n = ES.index(to)
        way = d if to > 0 else -d
        go(remote(cb.at[b, h], cb.at[b, h], zs_sem.at[h, f, n], zr_sem.at[h, f, n], dev(x, z + NZ + way, c)))

    def znext(h, e, f):
        if 0 <= e < 4:
            zsend(h, e, f, e + 1)
        if -3 < e <= 0:
            zsend(h, e, f, e - 1)

    def xsend(h, e):
        b, n = item(e, 0), ES.index(e)
        for w in range(2):
            who = dev(x + (1 if w == 0 else NX - 1), z, c)
            go(remote(cb.at[b, h], cb.at[b, h], hs_sem.at[h, n, w], hr_sem.at[h, n, w], who))

    def xnext(h, e, f):
        b, n, w = item(e, f), ES.index(e), f - 1
        piece = cb.at[b, h, pl.ds(HALF * w, HALF)]
        who = dev(x + (1 if w == 0 else NX - 1), z, c)
        go(remote(piece, piece, fs_sem.at[h, n, w], fr_sem.at[h, n, w], who))

    def take(h, e, f):
        b, n = item(e, f), ES.index(e)
        along_x = f > 0 and (h == 1 or e == 0)
        if along_x and f < 3:
            arrived(cb.at[b, h], hr_sem.at[h, n, f - 1])
        elif along_x:
            for w in range(2):
                arrived(cb.at[b, h, pl.ds(HALF * w, HALF)], fr_sem.at[h, n, w])
        elif e != 0:
            arrived(cb.at[b, h], zr_sem.at[h, f, n])
        if h == 1:
            if f == 0:
                znext(h, e, f)
                xsend(h, e)
            elif f < 3:
                xnext(h, e, f)
        else:
            if e == 0 and f == 0:
                xsend(h, e)
            if e == 0 and 0 < f < 3:
                xnext(h, e, f)
            znext(h, e, f)

    def cross(e, f):
        n = UNITS.index((e, f))
        b = item(e, f)
        go(remote(cb.at[b], cb.at[b], cs_sem.at[n], cr_sem.at[n], dev(x, z, 1 - c)))

    for l in range(3):
        t = tg[l].reshape(256, 512)
        for q in range(2):
            total = jnp.dot(t[:, 0:256], lvl[l, q], preferred_element_type=F32)
            for g in FILL[l][q]:
                near(g)
            arrived(part.at[l, q], br_sem.at[l, q])
            total = total + jnp.dot(t[:, 256:512], part[l, q], preferred_element_type=F32)
            if l < 2:
                lvl[l + 1, q] = total.astype(BF16)
                swap(l + 1, q).start()
            else:
                cb[leaf, q] = total.astype(BF16)
                take(q, 0, 0)
    cross(0, 0)

    lanes = lax.broadcasted_iota(jnp.int32, (1, HALF), 1)

    def quad(units):
        rows, wants = [], []
        for e, f in units:
            mirror = e if e in (0, 4) else -e
            n = UNITS.index((mirror, f))
            zz = (z + 2 * NZ - d * e) % NZ
            xx = (x + SHIFT[f]) % NX
            theirs = leaf_id(xx, zz, 1 - c)
            arrived(cb.at[theirs], cr_sem.at[n])
            b0 = leaf_id(xx, zz, 0)
            wants.append((lanes + b0 * CAP).astype(F32))
            for cc in range(2):
                coeff = jnp.concatenate([cb[b0 + cc, 0], cb[b0 + cc, 1]], axis=1)
                rows.append(jnp.dot(us[b0 + cc], coeff, preferred_element_type=F32).astype(BF16))
        far = jnp.concatenate(rows, axis=0)

        def back(i, carry):
            span = pl.ds(pl.multiple_of(i * 256, 256), 256)
            col = scol[span, :]
            hot = jnp.concatenate([(col == w).astype(F32).astype(BF16) for w in wants], axis=1)
            acc[span, :] = acc[span, :] + jnp.dot(hot, far, preferred_element_type=F32)
            return carry

        lax.fori_loop(0, ROWS // 256, back, 0)

    done = 0
    ready = 1
    for r in range(1, 7):
        for e, f in ROUNDS[r]:
            for h in range(2):
                take(h, e, f)
            cross(e, f)
        while done + 4 <= ready:
            quad(UNITS[done : done + 4])
            done += 4
        ready += len(ROUNDS[r])
    while done < len(UNITS):
        quad(UNITS[done : done + 4])
        done += 4
    out_ref[...] = acc[...].astype(BF16)

    for cp in sent:
        cp.wait_send()
    for cp in tcopies:
        cp.wait_send()
    for l in range(3):
        for q in range(2):
            swap(l, q).wait_send()
    for i in range(NZ):
        arrived(sx.at[i], xs_sem.at[i])
        arrived(sv.at[i], vs_sem.at[i])
        arrived(rv.at[i, pl.ds(1, NY - 1)], ys_sem.at[i])
    for s in range(NZ - 1):
        for q in range(2):
            ring_copy(s, q).wait_send()


def on_device(
    fields, owner, source_basis, field_basis, transfer, near_blocks, near_index, near_count
):
    vmem = pl.BlockSpec(memory_space=pltpu.VMEM)
    smem = pl.BlockSpec(memory_space=pltpu.SMEM)
    hbm = pl.BlockSpec(memory_space=pl.ANY)
    dma = pltpu.SemaphoreType.DMA
    return pl.pallas_call(
        whole_kernel,
        out_shape=jax.ShapeDtypeStruct((ROWS, 256), BF16),
        in_specs=[vmem, smem, smem, hbm, hbm, hbm, hbm, hbm],
        out_specs=vmem,
        scratch_shapes=[
            pltpu.VMEM((8, 256, 256), BF16),
            pltpu.VMEM((ROWS, 256), BF16),
            pltpu.VMEM((ROWS, 256), BF16),
            pltpu.VMEM((8, 7, 256, 256), BF16),
            pltpu.VMEM((1, ROWS), F32),
            pltpu.VMEM((ROWS, HALF), F32),
            pltpu.VMEM((NZ, NG - 1, NY, Q, 256), BF16),
            pltpu.VMEM((NZ, NG - 1, Q, 256), BF16),
            pltpu.VMEM((NZ, NY, NG, Q, 256), BF16),
            pltpu.VMEM((NZ, NY, NG, Q, 256), BF16),
            pltpu.VMEM((NB, CAP, 256), BF16),
            pltpu.VMEM((NZ, 2, 256, HALF), F32),
            pltpu.VMEM((3, 2, 256, HALF), BF16),
            pltpu.VMEM((3, 2, 256, HALF), BF16),
            pltpu.VMEM((3, NY, 64, 512), BF16),
            pltpu.VMEM((NB, 2, 256, HALF), BF16),
            pltpu.VMEM((ROWS, 256), F32),
            dma((4,)), dma((8,)),
            dma((NZ,)), dma((NZ,)), dma((NZ,)), dma((NZ,)), dma((NZ,)), dma((NZ,)),
            dma((NZ, 2)), dma((NZ, 2)), dma((3, 2)), dma((3, 2)), dma((3,)), dma((3,)),
            dma((2, 4, 8)), dma((2, 4, 8)),
            dma((2, 8, 2)), dma((2, 8, 2)),
            dma((2, 8, 2)), dma((2, 8, 2)),
            dma((32,)), dma((32,)),
        ],
        compiler_params=pltpu.CompilerParams(
            collective_id=0, has_side_effects=True, vmem_limit_bytes=63 * 1024 * 1024
        ),
    )(
        owner.reshape(1, -1), near_index, near_count, fields.reshape(8, 256, 256), source_basis, field_basis,
        transfer[0], near_blocks,
    )


def solution(mesh):
    in_specs = (
        P("leaf", "rhs"),
        P("leaf", None),
        P("leaf", None),
        P("leaf", None),
        P("leaf", None, "rhs", None),
        P("leaf", None, None, None),
        P("leaf", None),
        P("leaf"),
    )
    return jax.shard_map(
        on_device, mesh=mesh, in_specs=in_specs, out_specs=P("leaf", "rhs"), check_vma=False
    )
```

```python
import jax
import jax.numpy as jnp
from jax import lax
from jax.experimental import pallas as pl
from jax.experimental.pallas import tpu as pltpu
from jax.sharding import PartitionSpec as P

MESH = pl.DeviceIdType.MESH
F32 = jnp.float32
BF16 = jnp.bfloat16
CAP = 64
NX, NZ, NC, NY = 4, 8, 2, 4
NB = NX * NZ * NC
NG = NX * NC
Q = CAP // NY
ROWS = 2048
HALF = 128
ES = [0, 1, -1, 2, -2, 3, -3, 4]
DIST = [0, 1, 1, 2]
SHIFT = [0, NX - 1, 1, 2]
ROUNDS = [[(e, f) for e in ES for f in range(4) if abs(e) + DIST[f] == r] for r in range(7)]
UNITS = [u for r in ROUNDS for u in r]
LATE = [3, -3, 4]
ZSET = [(1, 0, n) for n in range(1, 8)]
ZSET += [(0, f, n) for f in range(4) for n in range(1, 8) if f < 3 or ES[n] not in LATE]
XSET = [(1, n, w) for n in range(8) for w in range(2)] + [(0, 0, 0), (0, 0, 1)]
FSET = [(1, n) for n in range(8)] + [(0, 0)] + [(0, ES.index(e)) for e in LATE]
SENT = (len(ZSET) + len(XSET) + len(FSET)) // 2 + len(UNITS)
FILL = [[[], []], [[3, 4], []], [[5, 6, 7], []]]


def leaf_id(x, z, c):
    return x * (NZ * NC) + z * NC + c


def whole_kernel(
    owner_ref, index_ref, count_ref, x_hbm, v_hbm, u_hbm, t_hbm, n_hbm, out_ref,
    xb, vb, ub, nb, slot, scol, sx, sv, rx, rv, us, ring, lvl, part, tg, cb, acc,
    in_sem, n_sem,
    xs_sem, xr_sem, vs_sem, vr_sem, ys_sem, yr_sem, rs_sem, rr_sem, bs_sem, br_sem, ts_sem, tr_sem,
    as_sem, zr_sem, hr_sem, fr_sem, cr_sem,
):
    leaf = lax.axis_index("leaf")
    y = lax.axis_index("rhs")
    x = leaf // (NZ * NC)
    z = (leaf // NC) % NZ
    c = leaf % NC
    d = 1 - 2 * c

    def dev(xx, zz, cc):
        return {"leaf": leaf_id(xx % NX, zz % NZ, cc), "rhs": y}

    def peer(k):
        return {"leaf": leaf, "rhs": (y + k) % NY}

    def remote(src, dst, ssem, rsem, who):
        return pltpu.make_async_remote_copy(
            src_ref=src, dst_ref=dst, send_sem=ssem, recv_sem=rsem,
            device_id=who, device_id_type=MESH,
        )

    def arrived(ref, sem):
        pltpu.make_async_copy(ref, ref, sem).wait()

    loads = [
        pltpu.make_async_copy(x_hbm, xb, in_sem.at[0]),
        pltpu.make_async_copy(v_hbm, vb, in_sem.at[1]),
        pltpu.make_async_copy(t_hbm, tg.at[:, y], in_sem.at[2]),
        pltpu.make_async_copy(u_hbm, ub, in_sem.at[3]),
    ]
    for cp in loads:
        cp.start()

    barrier = pltpu.get_barrier_semaphore()
    peers = [dev(x + dx, z, (c + dc) % NC) for dx in range(NX) for dc in range(NC) if dx or dc]
    z4 = (z // 4) * 4
    z2 = z4 + (z - z4 + 2) % 4
    z1 = (z // 2) * 2 + (1 - z % 2)
    peers += [dev(x, z + 1, c), dev(x, z + NZ - 1, c), dev(x, z2, c)]
    peers += [peer(k) for k in range(1, NY)]
    for who in peers:
        pl.semaphore_signal(barrier, inc=1, device_id=who, device_id_type=MESH)

    step = 256
    below = lax.broadcasted_iota(jnp.int32, (step, step), 0)
    above = lax.broadcasted_iota(jnp.int32, (step, step), 1)
    tri = (below < above).astype(F32).astype(BF16)
    carry = jnp.zeros((NB, 1), F32)
    names = lax.broadcasted_iota(jnp.int32, (NB, step), 0)
    for i in range(ROWS // step):
        own = owner_ref[:, i * step : (i + 1) * step]
        hot = (names == own).astype(F32)
        before = jnp.dot(hot.astype(BF16), tri, preferred_element_type=F32) + carry
        rank = jnp.sum(before * hot, axis=0, keepdims=True)
        slot[:, i * step : (i + 1) * step] = own.astype(F32) * CAP + rank
        carry = carry + jnp.sum(hot, axis=1, keepdims=True)

    pl.semaphore_wait(barrier, len(peers))
    for cp in loads[:3]:
        cp.wait()
    nload = pltpu.make_async_copy(n_hbm, nb, n_sem)
    nload.start()

    rel = lax.broadcasted_iota(jnp.int32, (CAP, 1), 0)
    ranks = ((y + NY - rel // Q) % NY) * Q + rel % Q

    def permute(i):
        slots = slot[...]
        hots = []
        for k in range(NG):
            xx, cc = (x + k // NC) % NX, (c + k % NC) % NC
            zz = (z + NZ - (1 - 2 * cc) * (i + 1)) % NZ
            want = (ranks + leaf_id(xx, zz, cc) * CAP).astype(F32)
            hots.append((slots == want).astype(F32).astype(BF16))
        quarter = jnp.concatenate([h[0:Q] for h in hots], axis=0)
        vp = jnp.dot(quarter, vb[...], preferred_element_type=F32).astype(BF16)
        rv[i, 0, 0] = vp[0:Q]
        sv[i] = vp[Q:].reshape(NG - 1, Q, 256)
        for k in range(1, NG):
            who = dev(x + k // NC, z, (c + k % NC) % NC)
            remote(sv.at[i, k - 1], rv.at[i, 0, k], vs_sem, vr_sem.at[i], who).start()
        xp = jnp.dot(jnp.concatenate(hots, axis=0), xb[...].reshape(ROWS, 256), preferred_element_type=F32).astype(BF16)
        rx[i, :, 0] = xp[0:CAP].reshape(NY, Q, 256)
        sx[i] = xp[CAP:].reshape(NG - 1, NY, Q, 256)
        for k in range(1, NG):
            who = dev(x + k // NC, z, (c + k % NC) % NC)
            remote(sx.at[i, k - 1], rx.at[i, :, k], xs_sem, xr_sem.at[i], who).start()

    def share(i):
        arrived(rv.at[i, 0, pl.ds(1, NG - 1)], vr_sem.at[i])
        for k in range(1, NY):
            remote(rv.at[i, 0], rv.at[i, k], ys_sem, yr_sem.at[i], peer(k)).start()

    def place(i):
        want = (lax.broadcasted_iota(jnp.int32, (8 * CAP, 1), 0) + i * (8 * CAP)).astype(F32)
        hot = (slot[...] == want).astype(F32).astype(BF16)
        up = jnp.dot(hot, ub[...], preferred_element_type=F32).astype(BF16)
        us[pl.ds(i * 8, 8)] = up.reshape(8, CAP, 256)

    def near(i):
        total = jnp.zeros((256, 256), F32)
        for j in range(7):
            keep = jnp.minimum(jnp.maximum(count_ref[i] - j, 0), 1).astype(F32)
            term = jnp.dot(nb[i, j], xb[index_ref[i, j]], preferred_element_type=F32)
            total = total + term * keep
        acc[i * 256 : i * 256 + 256, :] = total

    def product(i):
        arrived(rx.at[i, :, pl.ds(1, NG - 1)], xr_sem.at[i])
        arrived(rv.at[i, pl.ds(1, NY - 1)], yr_sem.at[i])
        vs = rv[i].reshape(NG * CAP, 256)
        xs = rx[i].reshape(NG * CAP, 256)
        return lax.dot_general(vs, xs, (((0,), (0,)), ((), ())), preferred_element_type=F32)

    nxt = dev(x, z + NZ + d, c)

    def ring_copy(s, q):
        return remote(ring.at[s, q], ring.at[s + 1, q], rs_sem, rr_sem.at[s, q], nxt)

    def ring_first():
        p = product(0)
        for q in range(2):
            ring[0, q] = p[:, HALF * q : HALF * q + HALF]
            ring_copy(0, q).start()

    def ring_step(s, between):
        p = product(s)
        for q in range(2):
            ring_copy(s - 1, q).wait_recv()
            ring[s, q] = ring[s, q] + p[:, HALF * q : HALF * q + HALF]
            ring_copy(s, q).start()
            if q == 0:
                between()

    def tsend(l):
        for k in range(1, NY):
            remote(tg.at[l, y], tg.at[l, y], ts_sem, tr_sem.at[l], peer(k)).start()

    tsend(0)
    permute(0)
    permute(1)
    share(0)
    loads[3].wait()
    permute(2)
    place(0)
    share(1)
    ring_first()
    permute(3)
    share(2)

    def step_on(m, carry):
        ring_step(m - 2, lambda: permute(m + 1))
        share(m)
        return carry

    lax.fori_loop(3, NZ - 1, step_on, 0)
    ring_step(NZ - 3, lambda: place(1))
    share(NZ - 1)
    tsend(1)
    tsend(2)
    ring_step(NZ - 2, lambda: place(2))

    mates = [dev(x, z, 1 - c), dev(x, z1, c), dev(x, z2, c)]

    def swap(l, q):
        return remote(lvl.at[l, q], part.at[l, q], bs_sem, br_sem.at[l, q], mates[l])

    last = product(NZ - 1)
    for q in range(2):
        ring_copy(NZ - 2, q).wait_recv()
        lvl[0, q] = (ring[NZ - 1, q] + last[:, HALF * q : HALF * q + HALF]).astype(BF16)
        swap(0, q).start()

    def go(cp):
        cp.start()

    def item(e, f):
        return leaf_id((x + SHIFT[f]) % NX, (z + 2 * NZ - d * e) % NZ, c)

    def zsend(h, e, f, to):
        b = item(e, f)
        n = ES.index(to)
        way = d if to > 0 else -d
        go(remote(cb.at[b, h], cb.at[b, h], as_sem, zr_sem.at[ZSET.index((h, f, n))], dev(x, z + NZ + way, c)))

    def znext(h, e, f):
        far_off = 2 if f == 3 else 4
        if 0 <= e < far_off:
            zsend(h, e, f, e + 1)
        if -min(far_off, 3) < e <= 0:
            zsend(h, e, f, e - 1)

    def xsend(h, e):
        b, n = item(e, 0), ES.index(e)
        for w in range(2):
            who = dev(x + (1 if w == 0 else NX - 1), z, c)
            go(remote(cb.at[b, h], cb.at[b, h], as_sem, hr_sem.at[XSET.index((h, n, w))], who))

    def xnext(h, e, f):
        b, n, w = item(e, f), ES.index(e), f - 1
        piece = cb.at[b, h, pl.ds(HALF * w, HALF)]
        who = dev(x + (1 if w == 0 else NX - 1), z, c)
        go(remote(piece, piece, as_sem, fr_sem.at[FSET.index((h, n))], who))

    def take(h, e, f):
        b, n = item(e, f), ES.index(e)
        along_x = f > 0 and (h == 1 or e == 0 or (f == 3 and e in LATE))
        if along_x and f < 3:
            arrived(cb.at[b, h], hr_sem.at[XSET.index((h, n, f - 1))])
        elif along_x:
            arrived(cb.at[b, h], fr_sem.at[FSET.index((h, n))])
        elif e != 0:
            arrived(cb.at[b, h], zr_sem.at[ZSET.index((h, f, n))])
        if h == 1:
            if f == 0:
                znext(h, e, f)
                xsend(h, e)
            elif f < 3:
                xnext(h, e, f)
        else:
            if e == 0 and f == 0:
                xsend(h, e)
            if (e == 0 or e in LATE) and 0 < f < 3:
                xnext(h, e, f)
            znext(h, e, f)

    def cross(e, f):
        n = UNITS.index((e, f))
        b = item(e, f)
        go(remote(cb.at[b], cb.at[b], as_sem, cr_sem.at[n], dev(x, z, 1 - c)))

    def columns():
        for i in range(ROWS // 128):
            row = jnp.broadcast_to(slot[:, i * 128 : (i + 1) * 128], (128, 128))
            scol[i * 128 : (i + 1) * 128, :] = jnp.transpose(row).astype(jnp.int32).astype(jnp.int16)

    for l in range(3):
        arrived(tg.at[l, pl.ds(0, NY - 1)], tr_sem.at[l])
        t = tg[l].reshape(256, 512)
        for q in range(2):
            total = jnp.dot(t[:, 0:256], lvl[l, q], preferred_element_type=F32)
            if (l, q) == (0, 0):
                columns()
            for g in FILL[l][q]:
                place(g)
            arrived(part.at[l, q], br_sem.at[l, q])
            total = total + jnp.dot(t[:, 256:512], part[l, q], preferred_element_type=F32)
            if l < 2:
                lvl[l + 1, q] = total.astype(BF16)
                swap(l + 1, q).start()
            else:
                cb[leaf, q] = total.astype(BF16)
                take(q, 0, 0)
    cross(0, 0)
    nload.wait()
    for g in range(6):
        near(g)

    lanes = lax.broadcasted_iota(jnp.int32, (16, HALF), 1)
    one, zero = jnp.ones((), BF16), jnp.zeros((), BF16)

    def quad(units):
        rows, wants = [], []
        for e, f in units:
            mirror = e if e in (0, 4) else -e
            n = UNITS.index((mirror, f))
            zz = (z + 2 * NZ - d * e) % NZ
            xx = (x + SHIFT[f]) % NX
            theirs = leaf_id(xx, zz, 1 - c)
            arrived(cb.at[theirs], cr_sem.at[n])
            b0 = leaf_id(xx, zz, 0)
            wants.append((lanes + b0 * CAP).astype(jnp.int16)[None])
            for cc in range(2):
                coeff = jnp.concatenate([cb[b0 + cc, 0], cb[b0 + cc, 1]], axis=1)
                rows.append(jnp.dot(us[b0 + cc], coeff, preferred_element_type=F32).astype(BF16))
        far = jnp.concatenate(rows, axis=0)

        col = scol[...].reshape(ROWS // 16, 16, HALF)
        hot = jnp.concatenate([jnp.where(col == w, one, zero).reshape(ROWS, HALF) for w in wants], axis=1)
        acc[...] = acc[...] + jnp.dot(hot, far, preferred_element_type=F32)

    done = 0
    ready = 1
    for r in range(1, 7):
        for e, f in ROUNDS[r]:
            for h in range(2):
                take(h, e, f)
            cross(e, f)
        if r == 1:
            near(6)
            near(7)
        while done + 4 <= ready:
            quad(UNITS[done : done + 4])
            done += 4
        ready += len(ROUNDS[r])
    while done < len(UNITS):
        quad(UNITS[done : done + 4])
        done += 4
    out_ref[...] = acc[...].astype(BF16)

    arrived(cb.at[pl.ds(0, SENT)], as_sem)
    arrived(tg.at[:, pl.ds(0, NY - 1)], ts_sem)
    arrived(lvl, bs_sem)
    arrived(sx, xs_sem)
    arrived(sv, vs_sem)
    arrived(rv.at[:, pl.ds(1, NY - 1)], ys_sem)
    arrived(ring.at[pl.ds(0, NZ - 1)], rs_sem)


def on_device(
    fields, owner, source_basis, field_basis, transfer, near_blocks, near_index, near_count
):
    vmem = pl.BlockSpec(memory_space=pltpu.VMEM)
    smem = pl.BlockSpec(memory_space=pltpu.SMEM)
    hbm = pl.BlockSpec(memory_space=pl.ANY)
    dma = pltpu.SemaphoreType.DMA
    return pl.pallas_call(
        whole_kernel,
        out_shape=jax.ShapeDtypeStruct((ROWS, 256), BF16),
        in_specs=[vmem, smem, smem, hbm, hbm, hbm, hbm, hbm],
        out_specs=vmem,
        scratch_shapes=[
            pltpu.VMEM((8, 256, 256), BF16),
            pltpu.VMEM((ROWS, 256), BF16),
            pltpu.VMEM((ROWS, 256), BF16),
            pltpu.VMEM((8, 7, 256, 256), BF16),
            pltpu.VMEM((1, ROWS), F32),
            pltpu.VMEM((ROWS, HALF), jnp.int16),
            pltpu.VMEM((NZ, NG - 1, NY, Q, 256), BF16),
            pltpu.VMEM((NZ, NG - 1, Q, 256), BF16),
            pltpu.VMEM((NZ, NY, NG, Q, 256), BF16),
            pltpu.VMEM((NZ, NY, NG, Q, 256), BF16),
            pltpu.VMEM((NB, CAP, 256), BF16),
            pltpu.VMEM((NZ, 2, 256, HALF), F32),
            pltpu.VMEM((3, 2, 256, HALF), BF16),
            pltpu.VMEM((3, 2, 256, HALF), BF16),
            pltpu.VMEM((3, NY, 64, 512), BF16),
            pltpu.VMEM((NB, 2, 256, HALF), BF16),
            pltpu.VMEM((ROWS, 256), F32),
            dma((4,)), dma(()),
            dma(()), dma((NZ,)), dma(()), dma((NZ,)), dma(()), dma((NZ,)),
            dma(()), dma((NZ, 2)), dma(()), dma((3, 2)), dma(()), dma((3,)),
            dma(()), dma((len(ZSET),)), dma((len(XSET),)), dma((len(FSET),)), dma((len(UNITS),)),
        ],
        compiler_params=pltpu.CompilerParams(
            collective_id=0, has_side_effects=True, vmem_limit_bytes=63 * 1024 * 1024
        ),
    )(
        owner.reshape(1, -1), near_index, near_count, fields.reshape(8, 256, 256), source_basis, field_basis,
        transfer[0], near_blocks,
    )


def solution(mesh):
    in_specs = (
        P("leaf", "rhs"),
        P("leaf", None),
        P("leaf", None),
        P("leaf", None),
        P("leaf", None, "rhs", None),
        P("leaf", None, None, None),
        P("leaf", None),
        P("leaf"),
    )
    return jax.shard_map(
        on_device, mesh=mesh, in_specs=in_specs, out_specs=P("leaf", "rhs"), check_vma=False
    )
```

```python
import jax
import jax.numpy as jnp
from jax import lax
from jax.experimental import pallas as pl
from jax.experimental.pallas import tpu as pltpu
from jax.sharding import PartitionSpec as P

MESH = pl.DeviceIdType.MESH
F32 = jnp.float32
BF16 = jnp.bfloat16
CAP = 64
NX, NZ, NC, NY = 4, 8, 2, 4
NB = NX * NZ * NC
NG = NX * NC
Q = CAP // NY
ROWS = 2048
HALF = 128
RING = F32
PIECES = [(0, 0), (HALF, 0), (0, HALF), (HALF, HALF)]
ES = [0, 1, -1, 2, -2, 3, -3, 4]
DIST = [0, 1, 1, 2]
SHIFT = [0, NX - 1, 1, 2]
ROUNDS = [[(e, f) for e in ES for f in range(4) if abs(e) + DIST[f] == r] for r in range(7)]
UNITS = [u for r in ROUNDS for u in r]
LATE = [3, -3, 4]
GROUPS = [[], [], [(0, 4)], [(4, 8), (8, 12)], [(12, 16), (16, 20)], [(20, 24), (24, 27)], [(27, 31), (31, 32)]]
ZSET = [(1, 0, n) for n in range(1, 8)]
ZSET += [(0, f, n) for f in range(4) for n in range(1, 8) if f < 3 or ES[n] not in LATE]
XSET = [(1, n, w) for n in range(8) for w in range(2)] + [(0, 0, 0), (0, 0, 1)]
FSET = [(1, n) for n in range(8)] + [(0, 0)] + [(0, ES.index(e)) for e in LATE]
SENT = (len(ZSET) + len(XSET) + len(FSET)) // 2 + len(UNITS)
FILL = [[[], []], [[3, 4], []], [[5, 6, 7], []]]


def leaf_id(x, z, c):
    return x * (NZ * NC) + z * NC + c


def whole_kernel(
    owner_ref, index_ref, count_ref, x_hbm, v_hbm, u_hbm, t_hbm, n_hbm, out_ref,
    xb, vb, ub, nb, slot, scol, sx, sv, rx, rv, us, ring, lvl, part, tg, cb, acc,
    in_sem, n_sem,
    xs_sem, xr_sem, vs_sem, vr_sem, ys_sem, yr_sem, rs_sem, rr_sem, bs_sem, br_sem, ts_sem, tr_sem,
    as_sem, zr_sem, hr_sem, fr_sem, cr_sem,
):
    leaf = lax.axis_index("leaf")
    y = lax.axis_index("rhs")
    x = leaf // (NZ * NC)
    z = (leaf // NC) % NZ
    c = leaf % NC
    d = 1 - 2 * c

    def dev(xx, zz, cc):
        return {"leaf": leaf_id(xx % NX, zz % NZ, cc), "rhs": y}

    def peer(k):
        return {"leaf": leaf, "rhs": (y + k) % NY}

    def remote(src, dst, ssem, rsem, who):
        return pltpu.make_async_remote_copy(
            src_ref=src, dst_ref=dst, send_sem=ssem, recv_sem=rsem,
            device_id=who, device_id_type=MESH,
        )

    def arrived(ref, sem):
        pltpu.make_async_copy(ref, ref, sem).wait()

    loads = [
        pltpu.make_async_copy(x_hbm, xb, in_sem.at[0]),
        pltpu.make_async_copy(v_hbm, vb, in_sem.at[1]),
        pltpu.make_async_copy(t_hbm, tg.at[:, y], in_sem.at[2]),
        pltpu.make_async_copy(u_hbm, ub, in_sem.at[3]),
    ]
    for cp in loads:
        cp.start()

    barrier = pltpu.get_barrier_semaphore()
    peers = [dev(x + dx, z, (c + dc) % NC) for dx in range(NX) for dc in range(NC) if dx or dc]
    z4 = (z // 4) * 4
    z2 = z4 + (z - z4 + 2) % 4
    z1 = (z // 2) * 2 + (1 - z % 2)
    peers += [dev(x, z + 1, c), dev(x, z + NZ - 1, c), dev(x, z2, c)]
    peers += [peer(k) for k in range(1, NY)]
    for who in peers:
        pl.semaphore_signal(barrier, inc=1, device_id=who, device_id_type=MESH)

    step = 256
    below = lax.broadcasted_iota(jnp.int32, (step, step), 0)
    above = lax.broadcasted_iota(jnp.int32, (step, step), 1)
    tri = (below < above).astype(F32).astype(BF16)
    carry = jnp.zeros((NB, 1), F32)
    names = lax.broadcasted_iota(jnp.int32, (NB, step), 0)
    for i in range(ROWS // step):
        own = owner_ref[:, i * step : (i + 1) * step]
        hot = (names == own).astype(F32)
        before = jnp.dot(hot.astype(BF16), tri, preferred_element_type=F32) + carry
        rank = jnp.sum(before * hot, axis=0, keepdims=True)
        slot[:, i * step : (i + 1) * step] = own.astype(F32) * CAP + rank
        carry = carry + jnp.sum(hot, axis=1, keepdims=True)

    pl.semaphore_wait(barrier, len(peers))
    for cp in loads[:3]:
        cp.wait()
    nload = pltpu.make_async_copy(n_hbm, nb, n_sem)
    nload.start()

    rel = lax.broadcasted_iota(jnp.int32, (CAP, 1), 0)
    ranks = ((y + NY - rel // Q) % NY) * Q + rel % Q

    def hots(i, ranks):
        slots = slot[...]
        rows = []
        for k in range(NG):
            xx, cc = (x + k // NC) % NX, (c + k % NC) % NC
            zz = (z + NZ - (1 - 2 * cc) * (i + 1)) % NZ
            want = (ranks + leaf_id(xx, zz, cc) * CAP).astype(F32)
            rows.append((slots == want).astype(F32).astype(BF16))
        return jnp.concatenate(rows, axis=0)

    def send_v(i):
        vp = jnp.dot(hots(i, ranks[0:Q]), vb[...], preferred_element_type=F32).astype(BF16)
        rv[i, 0, 0] = vp[0:Q]
        sv[i] = vp[Q:].reshape(NG - 1, Q, 256)
        for k in range(1, NG):
            who = dev(x + k // NC, z, (c + k % NC) % NC)
            remote(sv.at[i, k - 1], rv.at[i, 0, k], vs_sem, vr_sem.at[i], who).start()

    def send_x(i):
        xp = jnp.dot(hots(i, ranks), xb[...].reshape(ROWS, 256), preferred_element_type=F32).astype(BF16)
        rx[i, :, 0] = xp[0:CAP].reshape(NY, Q, 256)
        sx[i] = xp[CAP:].reshape(NG - 1, NY, Q, 256)
        for k in range(1, NG):
            who = dev(x + k // NC, z, (c + k % NC) % NC)
            remote(sx.at[i, k - 1], rx.at[i, :, k], xs_sem, xr_sem.at[i], who).start()

    def share(i):
        arrived(rv.at[i, 0, pl.ds(1, NG - 1)], vr_sem.at[i])
        for k in range(1, NY):
            remote(rv.at[i, 0], rv.at[i, k], ys_sem, yr_sem.at[i], peer(k)).start()

    def place(i):
        want = (lax.broadcasted_iota(jnp.int32, (8 * CAP, 1), 0) + i * (8 * CAP)).astype(F32)
        hot = (slot[...] == want).astype(F32).astype(BF16)
        up = jnp.dot(hot, ub[...], preferred_element_type=F32).astype(BF16)
        us[pl.ds(i * 8, 8)] = up.reshape(8, CAP, 256)

    def near(i):
        total = jnp.zeros((256, 256), F32)
        for j in range(7):
            keep = jnp.minimum(jnp.maximum(count_ref[i] - j, 0), 1).astype(F32)
            term = jnp.dot(nb[i, j], xb[index_ref[i, j]], preferred_element_type=F32)
            total = total + term * keep
        acc[i * 256 : i * 256 + 256, :] = total

    def product(i):
        arrived(rx.at[i, :, pl.ds(1, NG - 1)], xr_sem.at[i])
        arrived(rv.at[i, pl.ds(1, NY - 1)], yr_sem.at[i])
        vs = rv[i].reshape(NG * CAP, 256)
        xs = rx[i].reshape(NG * CAP, 256)
        return lax.dot_general(vs, xs, (((0,), (0,)), ((), ())), preferred_element_type=F32)

    nxt = dev(x, z + NZ + d, c)

    def ring_copy(s, q):
        return remote(ring.at[s, q], ring.at[s + 1, q], rs_sem, rr_sem.at[s, q], nxt)

    def piece(p, q):
        k, n = PIECES[q]
        return p[k : k + HALF, n : n + HALF]

    def ring_first():
        p = product(0)
        for q in range(4):
            ring[0, q] = piece(p, q).astype(RING)
            ring_copy(0, q).start()

    def ring_step(s, first, second):
        p = product(s)
        for q in range(4):
            ring_copy(s - 1, q).wait_recv()
            ring[s, q] = (ring[s, q].astype(F32) + piece(p, q)).astype(RING)
            ring_copy(s, q).start()
            if q == 0:
                first()
            if q == 2:
                second()

    def tsend(l):
        for k in range(1, NY):
            remote(tg.at[l, y], tg.at[l, y], ts_sem, tr_sem.at[l], peer(k)).start()

    tsend(0)
    send_v(0)
    send_x(0)
    send_v(1)
    share(0)
    send_x(1)
    send_v(2)
    loads[3].wait()
    place(0)
    share(1)
    send_x(2)
    send_v(3)
    ring_first()
    send_x(3)
    share(2)
    send_v(4)
    send_x(4)
    send_v(5)

    def step_on(m, carry):
        share(m)
        ring_step(m - 2, lambda: send_v(m + 3), lambda: send_x(m + 2))
        return carry

    def rest():
        return None

    lax.fori_loop(3, NZ - 3, step_on, 0)
    share(NZ - 3)
    ring_step(NZ - 5, rest, lambda: send_x(NZ - 1))
    share(NZ - 2)
    ring_step(NZ - 4, rest, lambda: place(1))
    share(NZ - 1)
    tsend(1)
    tsend(2)
    ring_step(NZ - 3, rest, lambda: place(2))
    ring_step(NZ - 2, rest, rest)

    mates = [dev(x, z, 1 - c), dev(x, z1, c), dev(x, z2, c)]

    def swap(l, q):
        return remote(lvl.at[l, q], part.at[l, q], bs_sem, br_sem.at[l, q], mates[l])

    last = product(NZ - 1)
    for q in range(2):
        for h in range(2):
            ring_copy(NZ - 2, 2 * q + h).wait_recv()
            total = ring[NZ - 1, 2 * q + h].astype(F32) + piece(last, 2 * q + h)
            lvl[0, q, HALF * h : HALF * h + HALF, :] = total.astype(BF16)
        swap(0, q).start()

    def go(cp):
        cp.start()

    def item(e, f):
        return leaf_id((x + SHIFT[f]) % NX, (z + 2 * NZ - d * e) % NZ, c)

    def zsend(h, e, f, to):
        b = item(e, f)
        n = ES.index(to)
        way = d if to > 0 else -d
        go(remote(cb.at[b, h], cb.at[b, h], as_sem, zr_sem.at[ZSET.index((h, f, n))], dev(x, z + NZ + way, c)))

    def znext(h, e, f):
        far_off = 2 if f == 3 else 4
        if 0 <= e < far_off:
            zsend(h, e, f, e + 1)
        if -min(far_off, 3) < e <= 0:
            zsend(h, e, f, e - 1)

    def xsend(h, e):
        b, n = item(e, 0), ES.index(e)
        for w in range(2):
            who = dev(x + (1 if w == 0 else NX - 1), z, c)
            go(remote(cb.at[b, h], cb.at[b, h], as_sem, hr_sem.at[XSET.index((h, n, w))], who))

    def xnext(h, e, f):
        b, n, w = item(e, f), ES.index(e), f - 1
        piece = cb.at[b, h, pl.ds(HALF * w, HALF)]
        who = dev(x + (1 if w == 0 else NX - 1), z, c)
        go(remote(piece, piece, as_sem, fr_sem.at[FSET.index((h, n))], who))

    def take(h, e, f):
        b, n = item(e, f), ES.index(e)
        along_x = f > 0 and (h == 1 or e == 0 or (f == 3 and e in LATE))
        if along_x and f < 3:
            arrived(cb.at[b, h], hr_sem.at[XSET.index((h, n, f - 1))])
        elif along_x:
            arrived(cb.at[b, h], fr_sem.at[FSET.index((h, n))])
        elif e != 0:
            arrived(cb.at[b, h], zr_sem.at[ZSET.index((h, f, n))])
        if h == 1:
            if f == 0:
                znext(h, e, f)
                xsend(h, e)
            elif f < 3:
                xnext(h, e, f)
        else:
            if e == 0 and f == 0:
                xsend(h, e)
            if (e == 0 or e in LATE) and 0 < f < 3:
                xnext(h, e, f)
            znext(h, e, f)

    def cross(e, f):
        n = UNITS.index((e, f))
        b = item(e, f)
        go(remote(cb.at[b], cb.at[b], as_sem, cr_sem.at[n], dev(x, z, 1 - c)))

    def columns():
        for i in range(ROWS // 128):
            row = jnp.broadcast_to(slot[:, i * 128 : (i + 1) * 128], (128, 128))
            scol[i * 128 : (i + 1) * 128, :] = jnp.transpose(row).astype(jnp.int32).astype(jnp.int16)

    for l in range(3):
        arrived(tg.at[l, pl.ds(0, NY - 1)], tr_sem.at[l])
        t = tg[l].reshape(256, 512)
        for q in range(2):
            total = jnp.dot(t[:, 0:256], lvl[l, q], preferred_element_type=F32)
            if (l, q) == (0, 0):
                columns()
            for g in FILL[l][q]:
                place(g)
            arrived(part.at[l, q], br_sem.at[l, q])
            total = total + jnp.dot(t[:, 256:512], part[l, q], preferred_element_type=F32)
            if l < 2:
                lvl[l + 1, q] = total.astype(BF16)
                swap(l + 1, q).start()
            else:
                cb[leaf, q] = total.astype(BF16)
                take(q, 0, 0)
    cross(0, 0)
    nload.wait()
    for g in range(6):
        near(g)

    lanes = lax.broadcasted_iota(jnp.int32, (16, HALF), 1)
    one, zero = jnp.ones((), BF16), jnp.zeros((), BF16)

    def quad(units):
        rows, wants = [], []
        for e, f in units:
            mirror = e if e in (0, 4) else -e
            n = UNITS.index((mirror, f))
            zz = (z + 2 * NZ - d * e) % NZ
            xx = (x + SHIFT[f]) % NX
            theirs = leaf_id(xx, zz, 1 - c)
            arrived(cb.at[theirs], cr_sem.at[n])
            b0 = leaf_id(xx, zz, 0)
            wants.append((lanes + b0 * CAP).astype(jnp.int16)[None])
            for cc in range(2):
                coeff = jnp.concatenate([cb[b0 + cc, 0], cb[b0 + cc, 1]], axis=1)
                rows.append(jnp.dot(us[b0 + cc], coeff, preferred_element_type=F32).astype(BF16))
        far = jnp.concatenate(rows, axis=0)

        def back(i, carry):
            span = pl.ds(pl.multiple_of(i * 1024, 1024), 1024)
            col = scol[span, :].reshape(1024 // 16, 16, HALF)
            hot = jnp.concatenate([jnp.where(col == w, one, zero).reshape(1024, HALF) for w in wants], axis=1)
            acc[span, :] = acc[span, :] + jnp.dot(hot, far, preferred_element_type=F32)
            return carry

        lax.fori_loop(0, ROWS // 1024, back, 0)

    for r in range(1, 7):
        for e, f in ROUNDS[r]:
            for h in range(2):
                take(h, e, f)
            cross(e, f)
        if r == 1:
            near(6)
            near(7)
        for lo, hi in GROUPS[r]:
            quad(UNITS[lo:hi])
    out_ref[...] = acc[...].astype(BF16)

    arrived(cb.at[pl.ds(0, SENT)], as_sem)
    arrived(tg.at[:, pl.ds(0, NY - 1)], ts_sem)
    arrived(lvl, bs_sem)
    arrived(sx, xs_sem)
    arrived(sv, vs_sem)
    arrived(rv.at[:, pl.ds(1, NY - 1)], ys_sem)
    arrived(ring.at[pl.ds(0, NZ - 1)], rs_sem)


def on_device(
    fields, owner, source_basis, field_basis, transfer, near_blocks, near_index, near_count
):
    vmem = pl.BlockSpec(memory_space=pltpu.VMEM)
    smem = pl.BlockSpec(memory_space=pltpu.SMEM)
    hbm = pl.BlockSpec(memory_space=pl.ANY)
    dma = pltpu.SemaphoreType.DMA
    return pl.pallas_call(
        whole_kernel,
        out_shape=pltpu.VMEM((ROWS, 256), BF16),
        in_specs=[vmem, smem, smem, hbm, hbm, hbm, hbm, hbm],
        out_specs=vmem,
        scratch_shapes=[
            pltpu.VMEM((8, 256, 256), BF16),
            pltpu.VMEM((ROWS, 256), BF16),
            pltpu.VMEM((ROWS, 256), BF16),
            pltpu.VMEM((8, 7, 256, 256), BF16),
            pltpu.VMEM((1, ROWS), F32),
            pltpu.VMEM((ROWS, HALF), jnp.int16),
            pltpu.VMEM((NZ, NG - 1, NY, Q, 256), BF16),
            pltpu.VMEM((NZ, NG - 1, Q, 256), BF16),
            pltpu.VMEM((NZ, NY, NG, Q, 256), BF16),
            pltpu.VMEM((NZ, NY, NG, Q, 256), BF16),
            pltpu.VMEM((NB, CAP, 256), BF16),
            pltpu.VMEM((NZ, 4, HALF, HALF), RING),
            pltpu.VMEM((3, 2, 256, HALF), BF16),
            pltpu.VMEM((3, 2, 256, HALF), BF16),
            pltpu.VMEM((3, NY, 64, 512), BF16),
            pltpu.VMEM((NB, 2, 256, HALF), BF16),
            pltpu.VMEM((ROWS, 256), F32),
            dma((4,)), dma(()),
            dma(()), dma((NZ,)), dma(()), dma((NZ,)), dma(()), dma((NZ,)),
            dma(()), dma((NZ - 1, 4)), dma(()), dma((3, 2)), dma(()), dma((3,)),
            dma(()), dma((len(ZSET),)), dma((len(XSET),)), dma((len(FSET),)), dma((len(UNITS),)),
        ],
        compiler_params=pltpu.CompilerParams(
            collective_id=0, has_side_effects=True, vmem_limit_bytes=58 * 1024 * 1024
        ),
    )(
        owner.reshape(1, -1), near_index, near_count, fields.reshape(8, 256, 256), source_basis, field_basis,
        transfer[0], near_blocks,
    )


def solution(mesh):
    in_specs = (
        P("leaf", "rhs"),
        P("leaf", None),
        P("leaf", None),
        P("leaf", None),
        P("leaf", None, "rhs", None),
        P("leaf", None, None, None),
        P("leaf", None),
        P("leaf"),
    )
    return jax.shard_map(
        on_device, mesh=mesh, in_specs=in_specs, out_specs=P("leaf", "rhs"), check_vma=False
    )
```

```python
import jax
import jax.numpy as jnp
from jax import lax
from jax.experimental import pallas as pl
from jax.experimental.pallas import tpu as pltpu
from jax.sharding import PartitionSpec as P

MESH = pl.DeviceIdType.MESH
F32 = jnp.float32
BF16 = jnp.bfloat16
CAP = 64
NX, NZ, NC, NY = 4, 8, 2, 4
NB = NX * NZ * NC
NG = NX * NC
Q = CAP // NY
ROWS = 2048
HALF = 128
RING = F32
PIECES = [(0, 0), (HALF, 0), (0, HALF), (HALF, HALF)]
ES = [0, 1, -1, 2, -2, 3, -3, 4]
DIST = [0, 1, 1, 2]
SHIFT = [0, NX - 1, 1, 2]
ROUNDS = [[(e, f) for e in ES for f in range(4) if abs(e) + DIST[f] == r] for r in range(7)]
UNITS = [u for r in ROUNDS for u in r]
LATE = [3, -3, 4]
GROUPS = {11: [(0, 4), (4, 8)], 19: [(8, 12), (12, 16)], 26: [(16, 20), (20, 24)]}
GROUPS.update({30: [(24, 27)], 31: [(27, 31), (31, 32)]})
ZSET = [(1, 0, n) for n in range(1, 8)]
ZSET += [(0, f, n) for f in range(4) for n in range(1, 8) if f < 3 or ES[n] not in LATE]
XSET = [(1, n, w) for n in range(8) for w in range(2)] + [(0, 0, 0), (0, 0, 1)]
FSET = [(1, n) for n in range(8)] + [(0, 0)] + [(0, ES.index(e)) for e in LATE]
SENT = (len(ZSET) + len(XSET) + len(FSET)) // 2 + len(UNITS)
FILL = [[[], []], [[3, 4], []], [[5, 6, 7], []]]


def leaf_id(x, z, c):
    return x * (NZ * NC) + z * NC + c


def whole_kernel(
    owner_ref, index_ref, count_ref, x_hbm, v_hbm, u_hbm, t_hbm, n_hbm, out_ref,
    xb, vb, ub, nb, slot, scol, sx, sv, rx, rv, us, ring, lvl, part, tg, cb, acc,
    in_sem, n_sem,
    xs_sem, xr_sem, vs_sem, vr_sem, ys_sem, yr_sem, rs_sem, rr_sem, bs_sem, br_sem, ts_sem, tr_sem,
    as_sem, zr_sem, hr_sem, fr_sem, cr_sem,
):
    leaf = lax.axis_index("leaf")
    y = lax.axis_index("rhs")
    x = leaf // (NZ * NC)
    z = (leaf // NC) % NZ
    c = leaf % NC
    d = 1 - 2 * c

    def dev(xx, zz, cc):
        return {"leaf": leaf_id(xx % NX, zz % NZ, cc), "rhs": y}

    def peer(k):
        return {"leaf": leaf, "rhs": (y + k) % NY}

    def remote(src, dst, ssem, rsem, who):
        return pltpu.make_async_remote_copy(
            src_ref=src, dst_ref=dst, send_sem=ssem, recv_sem=rsem,
            device_id=who, device_id_type=MESH,
        )

    def arrived(ref, sem):
        pltpu.make_async_copy(ref, ref, sem).wait()

    loads = [
        pltpu.make_async_copy(x_hbm, xb, in_sem.at[0]),
        pltpu.make_async_copy(v_hbm, vb, in_sem.at[1]),
        pltpu.make_async_copy(t_hbm, tg.at[:, y], in_sem.at[2]),
        pltpu.make_async_copy(u_hbm, ub, in_sem.at[3]),
    ]
    for cp in loads:
        cp.start()

    barrier = pltpu.get_barrier_semaphore()
    peers = [dev(x + dx, z, (c + dc) % NC) for dx in range(NX) for dc in range(NC) if dx or dc]
    z4 = (z // 4) * 4
    z2 = z4 + (z - z4 + 2) % 4
    z1 = (z // 2) * 2 + (1 - z % 2)
    peers += [dev(x, z + 1, c), dev(x, z + NZ - 1, c), dev(x, z2, c)]
    peers += [peer(k) for k in range(1, NY)]
    for who in peers:
        pl.semaphore_signal(barrier, inc=1, device_id=who, device_id_type=MESH)

    step = 256
    below = lax.broadcasted_iota(jnp.int32, (step, step), 0)
    above = lax.broadcasted_iota(jnp.int32, (step, step), 1)
    tri = (below < above).astype(F32).astype(BF16)
    carry = jnp.zeros((NB, 1), F32)
    names = lax.broadcasted_iota(jnp.int32, (NB, step), 0)
    for i in range(ROWS // step):
        own = owner_ref[:, i * step : (i + 1) * step]
        hot = (names == own).astype(F32)
        before = jnp.dot(hot.astype(BF16), tri, preferred_element_type=F32) + carry
        rank = jnp.sum(before * hot, axis=0, keepdims=True)
        slot[:, i * step : (i + 1) * step] = own.astype(F32) * CAP + rank
        carry = carry + jnp.sum(hot, axis=1, keepdims=True)

    pl.semaphore_wait(barrier, len(peers))
    for cp in loads[:3]:
        cp.wait()
    nload = pltpu.make_async_copy(n_hbm, nb, n_sem)
    nload.start()

    rel = lax.broadcasted_iota(jnp.int32, (CAP, 1), 0)
    ranks = ((y + NY - rel // Q) % NY) * Q + rel % Q

    def hots(i, ranks):
        slots = slot[...]
        rows = []
        for k in range(NG):
            xx, cc = (x + k // NC) % NX, (c + k % NC) % NC
            zz = (z + NZ - (1 - 2 * cc) * (i + 1)) % NZ
            want = (ranks + leaf_id(xx, zz, cc) * CAP).astype(F32)
            rows.append((slots == want).astype(F32).astype(BF16))
        return jnp.concatenate(rows, axis=0)

    def send_v(i):
        vp = jnp.dot(hots(i, ranks[0:Q]), vb[...], preferred_element_type=F32).astype(BF16)
        rv[i, 0, 0] = vp[0:Q]
        sv[i] = vp[Q:].reshape(NG - 1, Q, 256)
        for k in range(1, NG):
            who = dev(x + k // NC, z, (c + k % NC) % NC)
            remote(sv.at[i, k - 1], rv.at[i, 0, k], vs_sem, vr_sem.at[i], who).start()

    def send_x(i):
        xp = jnp.dot(hots(i, ranks), xb[...].reshape(ROWS, 256), preferred_element_type=F32).astype(BF16)
        rx[i, :, 0] = xp[0:CAP].reshape(NY, Q, 256)
        sx[i] = xp[CAP:].reshape(NG - 1, NY, Q, 256)
        for k in range(1, NG):
            who = dev(x + k // NC, z, (c + k % NC) % NC)
            remote(sx.at[i, k - 1], rx.at[i, :, k], xs_sem, xr_sem.at[i], who).start()

    def share(i):
        arrived(rv.at[i, 0, pl.ds(1, NG - 1)], vr_sem.at[i])
        for k in range(1, NY):
            remote(rv.at[i, 0], rv.at[i, k], ys_sem, yr_sem.at[i], peer(k)).start()

    def place(i):
        want = (lax.broadcasted_iota(jnp.int32, (8 * CAP, 1), 0) + i * (8 * CAP)).astype(F32)
        hot = (slot[...] == want).astype(F32).astype(BF16)
        up = jnp.dot(hot, ub[...], preferred_element_type=F32).astype(BF16)
        us[pl.ds(i * 8, 8)] = up.reshape(8, CAP, 256)

    def near(i):
        total = jnp.zeros((256, 256), F32)
        for j in range(7):
            keep = jnp.minimum(jnp.maximum(count_ref[i] - j, 0), 1).astype(F32)
            term = jnp.dot(nb[i, j], xb[index_ref[i, j]], preferred_element_type=F32)
            total = total + term * keep
        acc[i * 256 : i * 256 + 256, :] = total

    def product(i):
        arrived(rx.at[i, :, pl.ds(1, NG - 1)], xr_sem.at[i])
        arrived(rv.at[i, pl.ds(1, NY - 1)], yr_sem.at[i])
        vs = rv[i].reshape(NG * CAP, 256)
        xs = rx[i].reshape(NG * CAP, 256)
        return lax.dot_general(vs, xs, (((0,), (0,)), ((), ())), preferred_element_type=F32)

    nxt = dev(x, z + NZ + d, c)

    def ring_copy(s, q):
        return remote(ring.at[s, q], ring.at[s + 1, q], rs_sem, rr_sem.at[s, q], nxt)

    def piece(p, q):
        k, n = PIECES[q]
        return p[k : k + HALF, n : n + HALF]

    def ring_first():
        p = product(0)
        for q in range(4):
            ring[0, q] = piece(p, q).astype(RING)
            ring_copy(0, q).start()

    def ring_step(s, first, second):
        p = product(s)
        for q in range(4):
            ring_copy(s - 1, q).wait_recv()
            ring[s, q] = (ring[s, q].astype(F32) + piece(p, q)).astype(RING)
            ring_copy(s, q).start()
            if q == 0:
                first()
            if q == 2:
                second()

    def tsend(l):
        for k in range(1, NY):
            remote(tg.at[l, y], tg.at[l, y], ts_sem, tr_sem.at[l], peer(k)).start()

    tsend(0)
    send_v(0)
    send_x(0)
    send_v(1)
    share(0)
    send_x(1)
    send_v(2)
    loads[3].wait()
    place(0)
    share(1)
    send_x(2)
    send_v(3)
    ring_first()
    send_x(3)
    share(2)
    send_v(4)
    send_x(4)
    send_v(5)

    def step_on(m, carry):
        share(m)
        ring_step(m - 2, lambda: send_v(m + 3), lambda: send_x(m + 2))
        return carry

    def rest():
        return None

    lax.fori_loop(3, NZ - 3, step_on, 0)
    share(NZ - 3)
    ring_step(NZ - 5, rest, lambda: send_x(NZ - 1))
    share(NZ - 2)
    ring_step(NZ - 4, rest, lambda: place(1))
    share(NZ - 1)
    tsend(1)
    tsend(2)
    ring_step(NZ - 3, rest, lambda: place(2))
    ring_step(NZ - 2, rest, rest)

    mates = [dev(x, z, 1 - c), dev(x, z1, c), dev(x, z2, c)]

    def swap(l, q):
        return remote(lvl.at[l, q], part.at[l, q], bs_sem, br_sem.at[l, q], mates[l])

    last = product(NZ - 1)
    for q in range(2):
        for h in range(2):
            ring_copy(NZ - 2, 2 * q + h).wait_recv()
            total = ring[NZ - 1, 2 * q + h].astype(F32) + piece(last, 2 * q + h)
            lvl[0, q, HALF * h : HALF * h + HALF, :] = total.astype(BF16)
        swap(0, q).start()

    def go(cp):
        cp.start()

    def item(e, f):
        return leaf_id((x + SHIFT[f]) % NX, (z + 2 * NZ - d * e) % NZ, c)

    def zsend(h, e, f, to):
        b = item(e, f)
        n = ES.index(to)
        way = d if to > 0 else -d
        go(remote(cb.at[b, h], cb.at[b, h], as_sem, zr_sem.at[ZSET.index((h, f, n))], dev(x, z + NZ + way, c)))

    def znext(h, e, f):
        far_off = 2 if f == 3 else 4
        if 0 <= e < far_off:
            zsend(h, e, f, e + 1)
        if -min(far_off, 3) < e <= 0:
            zsend(h, e, f, e - 1)

    def xsend(h, e):
        b, n = item(e, 0), ES.index(e)
        for w in range(2):
            who = dev(x + (1 if w == 0 else NX - 1), z, c)
            go(remote(cb.at[b, h], cb.at[b, h], as_sem, hr_sem.at[XSET.index((h, n, w))], who))

    def xnext(h, e, f):
        b, n, w = item(e, f), ES.index(e), f - 1
        piece = cb.at[b, h, pl.ds(HALF * w, HALF)]
        who = dev(x + (1 if w == 0 else NX - 1), z, c)
        go(remote(piece, piece, as_sem, fr_sem.at[FSET.index((h, n))], who))

    def take(h, e, f):
        b, n = item(e, f), ES.index(e)
        along_x = f > 0 and (h == 1 or e == 0 or (f == 3 and e in LATE))
        if along_x and f < 3:
            arrived(cb.at[b, h], hr_sem.at[XSET.index((h, n, f - 1))])
        elif along_x:
            arrived(cb.at[b, h], fr_sem.at[FSET.index((h, n))])
        elif e != 0:
            arrived(cb.at[b, h], zr_sem.at[ZSET.index((h, f, n))])
        if h == 1:
            if f == 0:
                znext(h, e, f)
                xsend(h, e)
            elif f < 3:
                xnext(h, e, f)
        else:
            if e == 0 and f == 0:
                xsend(h, e)
            if (e == 0 or e in LATE) and 0 < f < 3:
                xnext(h, e, f)
            znext(h, e, f)

    def cross(e, f):
        n = UNITS.index((e, f))
        b = item(e, f)
        go(remote(cb.at[b], cb.at[b], as_sem, cr_sem.at[n], dev(x, z, 1 - c)))

    def columns():
        for i in range(ROWS // 128):
            row = jnp.broadcast_to(slot[:, i * 128 : (i + 1) * 128], (128, 128))
            scol[i * 128 : (i + 1) * 128, :] = jnp.transpose(row).astype(jnp.int32).astype(jnp.int16)

    for l in range(3):
        arrived(tg.at[l, pl.ds(0, NY - 1)], tr_sem.at[l])
        t = tg[l].reshape(256, 512)
        for q in range(2):
            total = jnp.dot(t[:, 0:256], lvl[l, q], preferred_element_type=F32)
            if (l, q) == (0, 0):
                columns()
            for g in FILL[l][q]:
                place(g)
            arrived(part.at[l, q], br_sem.at[l, q])
            total = total + jnp.dot(t[:, 256:512], part[l, q], preferred_element_type=F32)
            if l < 2:
                lvl[l + 1, q] = total.astype(BF16)
                swap(l + 1, q).start()
            else:
                cb[leaf, q] = total.astype(BF16)
                take(q, 0, 0)
    cross(0, 0)
    nload.wait()
    for g in range(6):
        near(g)

    lanes = lax.broadcasted_iota(jnp.int32, (16, HALF), 1)
    one, zero = jnp.ones((), BF16), jnp.zeros((), BF16)

    def quad(units):
        rows, wants = [], []
        for e, f in units:
            mirror = e if e in (0, 4) else -e
            n = UNITS.index((mirror, f))
            zz = (z + 2 * NZ - d * e) % NZ
            xx = (x + SHIFT[f]) % NX
            theirs = leaf_id(xx, zz, 1 - c)
            arrived(cb.at[theirs], cr_sem.at[n])
            b0 = leaf_id(xx, zz, 0)
            wants.append((lanes + b0 * CAP).astype(jnp.int16)[None])
            for cc in range(2):
                coeff = jnp.concatenate([cb[b0 + cc, 0], cb[b0 + cc, 1]], axis=1)
                rows.append(jnp.dot(us[b0 + cc], coeff, preferred_element_type=F32).astype(BF16))
        far = jnp.concatenate(rows, axis=0)

        def back(i, carry):
            span = pl.ds(pl.multiple_of(i * 1024, 1024), 1024)
            col = scol[span, :].reshape(1024 // 16, 16, HALF)
            hot = jnp.concatenate([jnp.where(col == w, one, zero).reshape(1024, HALF) for w in wants], axis=1)
            acc[span, :] = acc[span, :] + jnp.dot(hot, far, preferred_element_type=F32)
            return carry

        lax.fori_loop(0, ROWS // 1024, back, 0)

    n = 1
    for r in range(1, 7):
        for e, f in ROUNDS[r]:
            take(0, e, f)
        for e, f in ROUNDS[r]:
            take(1, e, f)
            cross(e, f)
        n += len(ROUNDS[r])
        if r == 1:
            near(6)
            near(7)
        for lo, hi in GROUPS.get(n - 1, []):
            quad(UNITS[lo:hi])
    out_ref[...] = acc[...].astype(BF16)

    arrived(cb.at[pl.ds(0, SENT)], as_sem)
    arrived(tg.at[:, pl.ds(0, NY - 1)], ts_sem)
    arrived(lvl, bs_sem)
    arrived(sx, xs_sem)
    arrived(sv, vs_sem)
    arrived(rv.at[:, pl.ds(1, NY - 1)], ys_sem)
    arrived(ring.at[pl.ds(0, NZ - 1)], rs_sem)


def on_device(
    fields, owner, source_basis, field_basis, transfer, near_blocks, near_index, near_count
):
    vmem = pl.BlockSpec(memory_space=pltpu.VMEM)
    smem = pl.BlockSpec(memory_space=pltpu.SMEM)
    hbm = pl.BlockSpec(memory_space=pl.ANY)
    dma = pltpu.SemaphoreType.DMA
    return pl.pallas_call(
        whole_kernel,
        out_shape=pltpu.VMEM((ROWS, 256), BF16),
        in_specs=[vmem, smem, smem, hbm, hbm, hbm, hbm, hbm],
        out_specs=vmem,
        scratch_shapes=[
            pltpu.VMEM((8, 256, 256), BF16),
            pltpu.VMEM((ROWS, 256), BF16),
            pltpu.VMEM((ROWS, 256), BF16),
            pltpu.VMEM((8, 7, 256, 256), BF16),
            pltpu.VMEM((1, ROWS), F32),
            pltpu.VMEM((ROWS, HALF), jnp.int16),
            pltpu.VMEM((NZ, NG - 1, NY, Q, 256), BF16),
            pltpu.VMEM((NZ, NG - 1, Q, 256), BF16),
            pltpu.VMEM((NZ, NY, NG, Q, 256), BF16),
            pltpu.VMEM((NZ, NY, NG, Q, 256), BF16),
            pltpu.VMEM((NB, CAP, 256), BF16),
            pltpu.VMEM((NZ, 4, HALF, HALF), RING),
            pltpu.VMEM((3, 2, 256, HALF), BF16),
            pltpu.VMEM((3, 2, 256, HALF), BF16),
            pltpu.VMEM((3, NY, 64, 512), BF16),
            pltpu.VMEM((NB, 2, 256, HALF), BF16),
            pltpu.VMEM((ROWS, 256), F32),
            dma((4,)), dma(()),
            dma(()), dma((NZ,)), dma(()), dma((NZ,)), dma(()), dma((NZ,)),
            dma(()), dma((NZ - 1, 4)), dma(()), dma((3, 2)), dma(()), dma((3,)),
            dma(()), dma((len(ZSET),)), dma((len(XSET),)), dma((len(FSET),)), dma((len(UNITS),)),
        ],
        compiler_params=pltpu.CompilerParams(
            collective_id=0, has_side_effects=True, vmem_limit_bytes=58 * 1024 * 1024
        ),
    )(
        owner.reshape(1, -1), near_index, near_count, fields.reshape(8, 256, 256), source_basis, field_basis,
        transfer[0], near_blocks,
    )


def solution(mesh):
    in_specs = (
        P("leaf", "rhs"),
        P("leaf", None),
        P("leaf", None),
        P("leaf", None),
        P("leaf", None, "rhs", None),
        P("leaf", None, None, None),
        P("leaf", None),
        P("leaf"),
    )
    return jax.shard_map(
        on_device, mesh=mesh, in_specs=in_specs, out_specs=P("leaf", "rhs"), check_vma=False
    )
```

```python
import jax
import jax.numpy as jnp
from jax import lax
from jax.experimental import pallas as pl
from jax.experimental.pallas import tpu as pltpu
from jax.sharding import PartitionSpec as P

MESH = pl.DeviceIdType.MESH
F32 = jnp.float32
BF16 = jnp.bfloat16
CAP = 64
NX, NZ, NC, NY = 4, 8, 2, 4
NB = NX * NZ * NC
NG = NX * NC
Q = CAP // NY
ROWS = 2048
HALF = 128
RING = BF16
PIECES = [(0, 0), (HALF, 0), (0, HALF), (HALF, HALF)]
ES = [0, 1, -1, 2, -2, 3, -3, 4]
DIST = [0, 1, 1, 2]
SHIFT = [0, NX - 1, 1, 2]
ROUNDS = [[(e, f) for e in ES for f in range(4) if abs(e) + DIST[f] == r] for r in range(7)]
UNITS = [u for r in ROUNDS for u in r]
LATE = [3, -3, 4]
GROUPS = {11: [(0, 4), (4, 8)], 19: [(8, 12), (12, 16)], 26: [(16, 20), (20, 24)]}
GROUPS.update({30: [(24, 27)], 31: [(27, 31), (31, 32)]})
ZSET = [(1, 0, n) for n in range(1, 8)]
ZSET += [(0, f, n) for f in range(4) for n in range(1, 8) if f < 3 or ES[n] not in LATE]
XSET = [(1, n, w) for n in range(8) for w in range(2)] + [(0, 0, 0), (0, 0, 1)]
FSET = [(1, n) for n in range(8)] + [(0, 0)] + [(0, ES.index(e)) for e in LATE]
SENT = (len(ZSET) + len(XSET) + len(FSET)) // 2 + len(UNITS)
FILL = [[[], []], [[3, 4], []], [[5, 6, 7], []]]


def leaf_id(x, z, c):
    return x * (NZ * NC) + z * NC + c


def whole_kernel(
    owner_ref, index_ref, count_ref, x_hbm, v_hbm, u_hbm, t_hbm, n_hbm, out_ref,
    xb, vb, ub, nb, slot, scol, sx, sv, rx, rv, us, ring, lvl, part, tg, cb, acc,
    in_sem, n_sem,
    xs_sem, xr_sem, vs_sem, vr_sem, ys_sem, yr_sem, rs_sem, rr_sem, bs_sem, br_sem, ts_sem, tr_sem,
    as_sem, zr_sem, hr_sem, fr_sem, cr_sem,
):
    leaf = lax.axis_index("leaf")
    y = lax.axis_index("rhs")
    x = leaf // (NZ * NC)
    z = (leaf // NC) % NZ
    c = leaf % NC
    d = 1 - 2 * c

    def dev(xx, zz, cc):
        return {"leaf": leaf_id(xx % NX, zz % NZ, cc), "rhs": y}

    def peer(k):
        return {"leaf": leaf, "rhs": (y + k) % NY}

    def remote(src, dst, ssem, rsem, who):
        return pltpu.make_async_remote_copy(
            src_ref=src, dst_ref=dst, send_sem=ssem, recv_sem=rsem,
            device_id=who, device_id_type=MESH,
        )

    def arrived(ref, sem):
        pltpu.make_async_copy(ref, ref, sem).wait()

    loads = [
        pltpu.make_async_copy(x_hbm, xb, in_sem.at[0]),
        pltpu.make_async_copy(v_hbm, vb, in_sem.at[1]),
        pltpu.make_async_copy(t_hbm, tg.at[:, y], in_sem.at[2]),
        pltpu.make_async_copy(u_hbm, ub, in_sem.at[3]),
    ]
    for cp in loads:
        cp.start()

    barrier = pltpu.get_barrier_semaphore()
    peers = [dev(x + dx, z, (c + dc) % NC) for dx in range(NX) for dc in range(NC) if dx or dc]
    z4 = (z // 4) * 4
    z2 = z4 + (z - z4 + 2) % 4
    z1 = (z // 2) * 2 + (1 - z % 2)
    peers += [dev(x, z + 1, c), dev(x, z + NZ - 1, c), dev(x, z2, c)]
    peers += [peer(k) for k in range(1, NY)]
    for who in peers:
        pl.semaphore_signal(barrier, inc=1, device_id=who, device_id_type=MESH)

    step = 256
    below = lax.broadcasted_iota(jnp.int32, (step, step), 0)
    above = lax.broadcasted_iota(jnp.int32, (step, step), 1)
    tri = (below < above).astype(F32).astype(BF16)
    carry = jnp.zeros((NB, 1), F32)
    names = lax.broadcasted_iota(jnp.int32, (NB, step), 0)
    for i in range(ROWS // step):
        own = owner_ref[:, i * step : (i + 1) * step]
        hot = (names == own).astype(F32)
        before = jnp.dot(hot.astype(BF16), tri, preferred_element_type=F32) + carry
        rank = jnp.sum(before * hot, axis=0, keepdims=True)
        slot[:, i * step : (i + 1) * step] = own.astype(F32) * CAP + rank
        carry = carry + jnp.sum(hot, axis=1, keepdims=True)

    pl.semaphore_wait(barrier, len(peers))
    for cp in loads[:3]:
        cp.wait()
    nload = pltpu.make_async_copy(n_hbm, nb, n_sem)
    nload.start()

    rel = lax.broadcasted_iota(jnp.int32, (CAP, 1), 0)
    ranks = ((y + NY - rel // Q) % NY) * Q + rel % Q

    def hots(i, ranks):
        slots = slot[...]
        rows = []
        for k in range(NG):
            xx, cc = (x + k // NC) % NX, (c + k % NC) % NC
            zz = (z + NZ - (1 - 2 * cc) * (i + 1)) % NZ
            want = (ranks + leaf_id(xx, zz, cc) * CAP).astype(F32)
            rows.append((slots == want).astype(F32).astype(BF16))
        return jnp.concatenate(rows, axis=0)

    def send_v(i):
        vp = jnp.dot(hots(i, ranks[0:Q]), vb[...], preferred_element_type=F32).astype(BF16)
        rv[i, 0, 0] = vp[0:Q]
        sv[i] = vp[Q:].reshape(NG - 1, Q, 256)
        for k in range(1, NG):
            who = dev(x + k // NC, z, (c + k % NC) % NC)
            remote(sv.at[i, k - 1], rv.at[i, 0, k], vs_sem, vr_sem.at[i], who).start()

    def send_x(i):
        xp = jnp.dot(hots(i, ranks), xb[...].reshape(ROWS, 256), preferred_element_type=F32).astype(BF16)
        rx[i, :, 0] = xp[0:CAP].reshape(NY, Q, 256)
        sx[i] = xp[CAP:].reshape(NG - 1, NY, Q, 256)
        for k in range(1, NG):
            who = dev(x + k // NC, z, (c + k % NC) % NC)
            remote(sx.at[i, k - 1], rx.at[i, :, k], xs_sem, xr_sem.at[i], who).start()

    def share(i):
        arrived(rv.at[i, 0, pl.ds(1, NG - 1)], vr_sem.at[i])
        for k in range(1, NY):
            remote(rv.at[i, 0], rv.at[i, k], ys_sem, yr_sem.at[i], peer(k)).start()

    def place(i):
        want = (lax.broadcasted_iota(jnp.int32, (8 * CAP, 1), 0) + i * (8 * CAP)).astype(F32)
        hot = (slot[...] == want).astype(F32).astype(BF16)
        up = jnp.dot(hot, ub[...], preferred_element_type=F32).astype(BF16)
        us[pl.ds(i * 8, 8)] = up.reshape(8, CAP, 256)

    def near(i):
        total = jnp.zeros((256, 256), F32)
        for j in range(7):
            keep = jnp.minimum(jnp.maximum(count_ref[i] - j, 0), 1).astype(F32)
            term = jnp.dot(nb[i, j], xb[index_ref[i, j]], preferred_element_type=F32)
            total = total + term * keep
        acc[i * 256 : i * 256 + 256, :] = total

    def product(i):
        arrived(rx.at[i, :, pl.ds(1, NG - 1)], xr_sem.at[i])
        arrived(rv.at[i, pl.ds(1, NY - 1)], yr_sem.at[i])
        vs = rv[i].reshape(NG * CAP, 256)
        xs = rx[i].reshape(NG * CAP, 256)
        return lax.dot_general(vs, xs, (((0,), (0,)), ((), ())), preferred_element_type=F32)

    nxt = dev(x, z + NZ + d, c)

    def ring_copy(s, q):
        return remote(ring.at[s, q], ring.at[s + 1, q], rs_sem, rr_sem.at[s, q], nxt)

    def piece(p, q):
        k, n = PIECES[q]
        return p[k : k + HALF, n : n + HALF]

    def ring_first():
        p = product(0)
        for q in range(4):
            ring[0, q] = piece(p, q).astype(RING)
            ring_copy(0, q).start()

    def ring_step(s, first, second):
        p = product(s)
        for q in range(4):
            ring_copy(s - 1, q).wait_recv()
            ring[s, q] = (ring[s, q].astype(F32) + piece(p, q)).astype(RING)
            ring_copy(s, q).start()
            if q == 0:
                first()
            if q == 2:
                second()

    def tsend(l):
        for k in range(1, NY):
            remote(tg.at[l, y], tg.at[l, y], ts_sem, tr_sem.at[l], peer(k)).start()

    tsend(0)
    send_v(0)
    send_x(0)
    send_v(1)
    share(0)
    send_x(1)
    send_v(2)
    loads[3].wait()
    place(0)
    share(1)
    send_x(2)
    send_v(3)
    ring_first()
    send_x(3)
    share(2)
    send_v(4)
    send_x(4)
    send_v(5)

    def step_on(m, carry):
        share(m)
        ring_step(m - 2, lambda: send_v(m + 3), lambda: send_x(m + 2))
        return carry

    def rest():
        return None

    lax.fori_loop(3, NZ - 3, step_on, 0)
    share(NZ - 3)
    ring_step(NZ - 5, rest, lambda: send_x(NZ - 1))
    share(NZ - 2)
    ring_step(NZ - 4, rest, lambda: place(1))
    share(NZ - 1)
    tsend(1)
    tsend(2)
    ring_step(NZ - 3, rest, lambda: place(2))
    ring_step(NZ - 2, rest, rest)

    mates = [dev(x, z, 1 - c), dev(x, z1, c), dev(x, z2, c)]

    def swap(l, q):
        return remote(lvl.at[l, q], part.at[l, q], bs_sem, br_sem.at[l, q], mates[l])

    last = product(NZ - 1)
    for q in range(2):
        for h in range(2):
            ring_copy(NZ - 2, 2 * q + h).wait_recv()
            total = ring[NZ - 1, 2 * q + h].astype(F32) + piece(last, 2 * q + h)
            lvl[0, q, HALF * h : HALF * h + HALF, :] = total.astype(BF16)
        swap(0, q).start()

    def go(cp):
        cp.start()

    def item(e, f):
        return leaf_id((x + SHIFT[f]) % NX, (z + 2 * NZ - d * e) % NZ, c)

    def zsend(h, e, f, to):
        b = item(e, f)
        n = ES.index(to)
        way = d if to > 0 else -d
        go(remote(cb.at[b, h], cb.at[b, h], as_sem, zr_sem.at[ZSET.index((h, f, n))], dev(x, z + NZ + way, c)))

    def znext(h, e, f):
        far_off = 2 if f == 3 else 4
        if 0 <= e < far_off:
            zsend(h, e, f, e + 1)
        if -min(far_off, 3) < e <= 0:
            zsend(h, e, f, e - 1)

    def xsend(h, e):
        b, n = item(e, 0), ES.index(e)
        for w in range(2):
            who = dev(x + (1 if w == 0 else NX - 1), z, c)
            go(remote(cb.at[b, h], cb.at[b, h], as_sem, hr_sem.at[XSET.index((h, n, w))], who))

    def xnext(h, e, f):
        b, n, w = item(e, f), ES.index(e), f - 1
        piece = cb.at[b, h, pl.ds(HALF * w, HALF)]
        who = dev(x + (1 if w == 0 else NX - 1), z, c)
        go(remote(piece, piece, as_sem, fr_sem.at[FSET.index((h, n))], who))

    def take(h, e, f):
        b, n = item(e, f), ES.index(e)
        along_x = f > 0 and (h == 1 or e == 0 or (f == 3 and e in LATE))
        if along_x and f < 3:
            arrived(cb.at[b, h], hr_sem.at[XSET.index((h, n, f - 1))])
        elif along_x:
            arrived(cb.at[b, h], fr_sem.at[FSET.index((h, n))])
        elif e != 0:
            arrived(cb.at[b, h], zr_sem.at[ZSET.index((h, f, n))])
        if h == 1:
            if f == 0:
                znext(h, e, f)
                xsend(h, e)
            elif f < 3:
                xnext(h, e, f)
        else:
            if e == 0 and f == 0:
                xsend(h, e)
            if (e == 0 or e in LATE) and 0 < f < 3:
                xnext(h, e, f)
            znext(h, e, f)

    def cross(e, f):
        n = UNITS.index((e, f))
        b = item(e, f)
        go(remote(cb.at[b], cb.at[b], as_sem, cr_sem.at[n], dev(x, z, 1 - c)))

    def columns():
        for i in range(ROWS // 128):
            row = jnp.broadcast_to(slot[:, i * 128 : (i + 1) * 128], (128, 128))
            scol[i * 128 : (i + 1) * 128, :] = jnp.transpose(row).astype(jnp.int32).astype(jnp.int16)

    for l in range(3):
        arrived(tg.at[l, pl.ds(0, NY - 1)], tr_sem.at[l])
        t = tg[l].reshape(256, 512)
        for q in range(2):
            total = jnp.dot(t[:, 0:256], lvl[l, q], preferred_element_type=F32)
            if (l, q) == (0, 0):
                columns()
            for g in FILL[l][q]:
                place(g)
            arrived(part.at[l, q], br_sem.at[l, q])
            total = total + jnp.dot(t[:, 256:512], part[l, q], preferred_element_type=F32)
            if l < 2:
                lvl[l + 1, q] = total.astype(BF16)
                swap(l + 1, q).start()
            else:
                cb[leaf, q] = total.astype(BF16)
                take(q, 0, 0)
    cross(0, 0)
    nload.wait()
    for g in range(6):
        near(g)

    lanes = lax.broadcasted_iota(jnp.int32, (16, HALF), 1)
    one, zero = jnp.ones((), BF16), jnp.zeros((), BF16)

    def quad(units):
        rows, wants = [], []
        for e, f in units:
            mirror = e if e in (0, 4) else -e
            n = UNITS.index((mirror, f))
            zz = (z + 2 * NZ - d * e) % NZ
            xx = (x + SHIFT[f]) % NX
            theirs = leaf_id(xx, zz, 1 - c)
            arrived(cb.at[theirs], cr_sem.at[n])
            b0 = leaf_id(xx, zz, 0)
            wants.append((lanes + b0 * CAP).astype(jnp.int16)[None])
            for cc in range(2):
                coeff = jnp.concatenate([cb[b0 + cc, 0], cb[b0 + cc, 1]], axis=1)
                rows.append(jnp.dot(us[b0 + cc], coeff, preferred_element_type=F32).astype(BF16))
        far = jnp.concatenate(rows, axis=0)

        def back(i, carry):
            span = pl.ds(pl.multiple_of(i * 1024, 1024), 1024)
            col = scol[span, :].reshape(1024 // 16, 16, HALF)
            hot = jnp.concatenate([jnp.where(col == w, one, zero).reshape(1024, HALF) for w in wants], axis=1)
            acc[span, :] = acc[span, :] + jnp.dot(hot, far, preferred_element_type=F32)
            return carry

        lax.fori_loop(0, ROWS // 1024, back, 0)

    n = 1
    for r in range(1, 7):
        for e, f in ROUNDS[r]:
            take(0, e, f)
        for e, f in ROUNDS[r]:
            take(1, e, f)
            cross(e, f)
        n += len(ROUNDS[r])
        if r == 1:
            near(6)
            near(7)
        for lo, hi in GROUPS.get(n - 1, []):
            quad(UNITS[lo:hi])
    out_ref[...] = acc[...].astype(BF16)

    arrived(cb.at[pl.ds(0, SENT)], as_sem)
    arrived(tg.at[:, pl.ds(0, NY - 1)], ts_sem)
    arrived(lvl, bs_sem)
    arrived(sx, xs_sem)
    arrived(sv, vs_sem)
    arrived(rv.at[:, pl.ds(1, NY - 1)], ys_sem)
    arrived(ring.at[pl.ds(0, NZ - 1)], rs_sem)


def on_device(
    fields, owner, source_basis, field_basis, transfer, near_blocks, near_index, near_count
):
    vmem = pl.BlockSpec(memory_space=pltpu.VMEM)
    smem = pl.BlockSpec(memory_space=pltpu.SMEM)
    hbm = pl.BlockSpec(memory_space=pl.ANY)
    dma = pltpu.SemaphoreType.DMA
    return pl.pallas_call(
        whole_kernel,
        out_shape=pltpu.VMEM((ROWS, 256), BF16),
        in_specs=[vmem, smem, smem, hbm, hbm, hbm, hbm, hbm],
        out_specs=vmem,
        scratch_shapes=[
            pltpu.VMEM((8, 256, 256), BF16),
            pltpu.VMEM((ROWS, 256), BF16),
            pltpu.VMEM((ROWS, 256), BF16),
            pltpu.VMEM((8, 7, 256, 256), BF16),
            pltpu.VMEM((1, ROWS), F32),
            pltpu.VMEM((ROWS, HALF), jnp.int16),
            pltpu.VMEM((NZ, NG - 1, NY, Q, 256), BF16),
            pltpu.VMEM((NZ, NG - 1, Q, 256), BF16),
            pltpu.VMEM((NZ, NY, NG, Q, 256), BF16),
            pltpu.VMEM((NZ, NY, NG, Q, 256), BF16),
            pltpu.VMEM((NB, CAP, 256), BF16),
            pltpu.VMEM((NZ, 4, HALF, HALF), RING),
            pltpu.VMEM((3, 2, 256, HALF), BF16),
            pltpu.VMEM((3, 2, 256, HALF), BF16),
            pltpu.VMEM((3, NY, 64, 512), BF16),
            pltpu.VMEM((NB, 2, 256, HALF), BF16),
            pltpu.VMEM((ROWS, 256), F32),
            dma((4,)), dma(()),
            dma(()), dma((NZ,)), dma(()), dma((NZ,)), dma(()), dma((NZ,)),
            dma(()), dma((NZ - 1, 4)), dma(()), dma((3, 2)), dma(()), dma((3,)),
            dma(()), dma((len(ZSET),)), dma((len(XSET),)), dma((len(FSET),)), dma((len(UNITS),)),
        ],
        compiler_params=pltpu.CompilerParams(
            collective_id=0, has_side_effects=True, vmem_limit_bytes=58 * 1024 * 1024
        ),
    )(
        owner.reshape(1, -1), near_index, near_count, fields.reshape(8, 256, 256), source_basis, field_basis,
        transfer[0], near_blocks,
    )


def solution(mesh):
    in_specs = (
        P("leaf", "rhs"),
        P("leaf", None),
        P("leaf", None),
        P("leaf", None),
        P("leaf", None, "rhs", None),
        P("leaf", None, None, None),
        P("leaf", None),
        P("leaf"),
    )
    return jax.shard_map(
        on_device, mesh=mesh, in_specs=in_specs, out_specs=P("leaf", "rhs"), check_vma=False
    )
```

```python
import jax
import jax.numpy as jnp
from jax import lax
from jax.experimental import pallas as pl
from jax.experimental.pallas import tpu as pltpu
from jax.sharding import PartitionSpec as P

MESH = pl.DeviceIdType.MESH
F32 = jnp.float32
BF16 = jnp.bfloat16
CAP = 64
NX, NZ, NC, NY = 4, 8, 2, 4
NB = NX * NZ * NC
NG = NX * NC
Q = CAP // NY
ROWS = 2048
HALF = 128
RING = F32
PIECES = [(0, 0), (HALF, 0), (0, HALF), (HALF, HALF)]
ES = [0, 1, -1, 2, -2, 3, -3, 4]
DIST = [0, 1, 1, 2]
SHIFT = [0, NX - 1, 1, 2]
ROUNDS = [[(e, f) for e in ES for f in range(4) if abs(e) + DIST[f] == r] for r in range(7)]
UNITS = [u for r in ROUNDS for u in r]
LATE = [3, -3, 4]
GROUPS = {11: [(0, 4), (4, 8)], 19: [(8, 12), (12, 16)], 26: [(16, 20), (20, 24)]}
GROUPS.update({30: [(24, 27)], 31: [(27, 31), (31, 32)]})
ZSET = [(1, 0, n) for n in range(1, 8)]
ZSET += [(0, f, n) for f in range(4) for n in range(1, 8) if f < 3 or ES[n] not in LATE]
XSET = [(1, n, w) for n in range(8) for w in range(2)] + [(0, 0, 0), (0, 0, 1)]
FSET = [(1, n) for n in range(8)] + [(0, 0)] + [(0, ES.index(e)) for e in LATE]
SENT = (len(ZSET) + len(XSET) + len(FSET)) // 2 + len(UNITS)
FILL = [[[], []], [[1, 2, 3], []], [[4, 5, 6, 7], []]]


def leaf_id(x, z, c):
    return x * (NZ * NC) + z * NC + c


def whole_kernel(
    owner_ref, index_ref, count_ref, x_hbm, v_hbm, u_hbm, t_hbm, n_hbm, out_ref,
    xb, vb, ub, nb, slot, scol, sx, sv, rx, rv, us, ring, lvl, part, tg, cb, acc,
    in_sem, n_sem,
    xs_sem, xr_sem, vs_sem, vr_sem, ys_sem, yr_sem, rs_sem, rr_sem, bs_sem, br_sem, ts_sem, tr_sem,
    as_sem, zr_sem, hr_sem, fr_sem, cr_sem,
):
    leaf = lax.axis_index("leaf")
    y = lax.axis_index("rhs")
    x = leaf // (NZ * NC)
    z = (leaf // NC) % NZ
    c = leaf % NC
    d = 1 - 2 * c

    def dev(xx, zz, cc):
        return {"leaf": leaf_id(xx % NX, zz % NZ, cc), "rhs": y}

    def peer(k):
        return {"leaf": leaf, "rhs": (y + k) % NY}

    def remote(src, dst, ssem, rsem, who):
        return pltpu.make_async_remote_copy(
            src_ref=src, dst_ref=dst, send_sem=ssem, recv_sem=rsem,
            device_id=who, device_id_type=MESH,
        )

    def arrived(ref, sem):
        pltpu.make_async_copy(ref, ref, sem).wait()

    loads = [
        pltpu.make_async_copy(x_hbm, xb, in_sem.at[0]),
        pltpu.make_async_copy(v_hbm, vb, in_sem.at[1]),
        pltpu.make_async_copy(t_hbm, tg.at[:, y], in_sem.at[2]),
        pltpu.make_async_copy(u_hbm, ub, in_sem.at[3]),
    ]
    for cp in loads:
        cp.start()

    barrier = pltpu.get_barrier_semaphore()
    peers = [dev(x + dx, z, (c + dc) % NC) for dx in range(NX) for dc in range(NC) if dx or dc]
    z4 = (z // 4) * 4
    z2 = z4 + (z - z4 + 2) % 4
    z1 = (z // 2) * 2 + (1 - z % 2)
    peers += [dev(x, z + 1, c), dev(x, z + NZ - 1, c), dev(x, z2, c)]
    peers += [peer(k) for k in range(1, NY)]
    for who in peers:
        pl.semaphore_signal(barrier, inc=1, device_id=who, device_id_type=MESH)

    step = 256
    below = lax.broadcasted_iota(jnp.int32, (step, step), 0)
    above = lax.broadcasted_iota(jnp.int32, (step, step), 1)
    tri = (below < above).astype(F32).astype(BF16)
    carry = jnp.zeros((NB, 1), F32)
    names = lax.broadcasted_iota(jnp.int32, (NB, step), 0)
    for i in range(ROWS // step):
        own = owner_ref[:, i * step : (i + 1) * step]
        hot = (names == own).astype(F32)
        before = jnp.dot(hot.astype(BF16), tri, preferred_element_type=F32) + carry
        rank = jnp.sum(before * hot, axis=0, keepdims=True)
        slot[:, i * step : (i + 1) * step] = own.astype(F32) * CAP + rank
        carry = carry + jnp.sum(hot, axis=1, keepdims=True)

    pl.semaphore_wait(barrier, len(peers))
    for cp in loads[:3]:
        cp.wait()
    nload = pltpu.make_async_copy(n_hbm, nb, n_sem)
    nload.start()

    rel = lax.broadcasted_iota(jnp.int32, (CAP, 1), 0)
    ranks = ((y + NY - rel // Q) % NY) * Q + rel % Q

    def hots(i, ranks):
        slots = slot[...]
        rows = []
        for k in range(NG):
            xx, cc = (x + k // NC) % NX, (c + k % NC) % NC
            zz = (z + NZ - (1 - 2 * cc) * (i + 1)) % NZ
            want = (ranks + leaf_id(xx, zz, cc) * CAP).astype(F32)
            rows.append((slots == want).astype(F32).astype(BF16))
        return jnp.concatenate(rows, axis=0)

    def send_v(i):
        vp = jnp.dot(hots(i, ranks[0:Q]), vb[...], preferred_element_type=F32).astype(BF16)
        rv[i, 0, 0] = vp[0:Q]
        sv[i] = vp[Q:].reshape(NG - 1, Q, 256)
        for k in range(1, NG):
            who = dev(x + k // NC, z, (c + k % NC) % NC)
            remote(sv.at[i, k - 1], rv.at[i, 0, k], vs_sem, vr_sem.at[i], who).start()

    def send_x(i):
        xp = jnp.dot(hots(i, ranks), xb[...].reshape(ROWS, 256), preferred_element_type=F32).astype(BF16)
        rx[i, :, 0] = xp[0:CAP].reshape(NY, Q, 256)
        sx[i] = xp[CAP:].reshape(NG - 1, NY, Q, 256)
        for k in range(1, NG):
            who = dev(x + k // NC, z, (c + k % NC) % NC)
            remote(sx.at[i, k - 1], rx.at[i, :, k], xs_sem, xr_sem.at[i], who).start()

    def share(i):
        arrived(rv.at[i, 0, pl.ds(1, NG - 1)], vr_sem.at[i])
        for k in range(1, NY):
            remote(rv.at[i, 0], rv.at[i, k], ys_sem, yr_sem.at[i], peer(k)).start()

    def place(i):
        want = (lax.broadcasted_iota(jnp.int32, (8 * CAP, 1), 0) + i * (8 * CAP)).astype(F32)
        hot = (slot[...] == want).astype(F32).astype(BF16)
        up = jnp.dot(hot, ub[...], preferred_element_type=F32).astype(BF16)
        us[pl.ds(i * 8, 8)] = up.reshape(8, CAP, 256)

    def near(i):
        total = jnp.zeros((256, 256), F32)
        for j in range(7):
            keep = jnp.minimum(jnp.maximum(count_ref[i] - j, 0), 1).astype(F32)
            term = jnp.dot(nb[i, j], xb[index_ref[i, j]], preferred_element_type=F32)
            total = total + term * keep
        acc[i * 256 : i * 256 + 256, :] = total

    def product(i):
        arrived(rx.at[i, :, pl.ds(1, NG - 1)], xr_sem.at[i])
        arrived(rv.at[i, pl.ds(1, NY - 1)], yr_sem.at[i])
        vs = rv[i].reshape(NG * CAP, 256)
        xs = rx[i].reshape(NG * CAP, 256)
        return lax.dot_general(vs, xs, (((0,), (0,)), ((), ())), preferred_element_type=F32)

    nxt = dev(x, z + NZ + d, c)

    def ring_copy(s, q):
        return remote(ring.at[s, q], ring.at[s + 1, q], rs_sem, rr_sem.at[s, q], nxt)

    def piece(p, q):
        k, n = PIECES[q]
        return p[k : k + HALF, n : n + HALF]

    def ring_first():
        p = product(0)
        for q in range(4):
            ring[0, q] = piece(p, q).astype(RING)
            ring_copy(0, q).start()

    def ring_step(s, first, second):
        p = product(s)
        for q in range(4):
            ring_copy(s - 1, q).wait_recv()
            ring[s, q] = (ring[s, q].astype(F32) + piece(p, q)).astype(RING)
            ring_copy(s, q).start()
            if q == 0:
                first()
            if q == 2:
                second()

    def tsend(l):
        for k in range(1, NY):
            remote(tg.at[l, y], tg.at[l, y], ts_sem, tr_sem.at[l], peer(k)).start()

    tsend(0)
    send_v(0)
    send_x(0)
    send_v(1)
    share(0)
    send_x(1)
    send_v(2)
    loads[3].wait()
    place(0)
    share(1)
    send_x(2)
    send_v(3)
    ring_first()
    send_x(3)
    share(2)
    send_v(4)
    send_x(4)
    send_v(5)

    def step_on(m, carry):
        share(m)
        ring_step(m - 2, lambda: send_v(m + 3), lambda: send_x(m + 2))
        return carry

    def rest():
        return None

    lax.fori_loop(3, NZ - 3, step_on, 0)
    share(NZ - 3)
    ring_step(NZ - 5, rest, lambda: send_x(NZ - 1))
    share(NZ - 2)
    ring_step(NZ - 4, rest, rest)
    share(NZ - 1)
    tsend(1)
    tsend(2)
    ring_step(NZ - 3, rest, rest)
    ring_step(NZ - 2, rest, rest)

    mates = [dev(x, z, 1 - c), dev(x, z1, c), dev(x, z2, c)]

    def swap(l, q):
        return remote(lvl.at[l, q], part.at[l, q], bs_sem, br_sem.at[l, q], mates[l])

    last = product(NZ - 1)
    for q in range(2):
        for h in range(2):
            ring_copy(NZ - 2, 2 * q + h).wait_recv()
            total = ring[NZ - 1, 2 * q + h].astype(F32) + piece(last, 2 * q + h)
            lvl[0, q, HALF * h : HALF * h + HALF, :] = total.astype(BF16)
        swap(0, q).start()

    def go(cp):
        cp.start()

    def item(e, f):
        return leaf_id((x + SHIFT[f]) % NX, (z + 2 * NZ - d * e) % NZ, c)

    def zsend(h, e, f, to):
        b = item(e, f)
        n = ES.index(to)
        way = d if to > 0 else -d
        go(remote(cb.at[b, h], cb.at[b, h], as_sem, zr_sem.at[ZSET.index((h, f, n))], dev(x, z + NZ + way, c)))

    def znext(h, e, f):
        far_off = 2 if f == 3 else 4
        if 0 <= e < far_off:
            zsend(h, e, f, e + 1)
        if -min(far_off, 3) < e <= 0:
            zsend(h, e, f, e - 1)

    def xsend(h, e):
        b, n = item(e, 0), ES.index(e)
        for w in range(2):
            who = dev(x + (1 if w == 0 else NX - 1), z, c)
            go(remote(cb.at[b, h], cb.at[b, h], as_sem, hr_sem.at[XSET.index((h, n, w))], who))

    def xnext(h, e, f):
        b, n, w = item(e, f), ES.index(e), f - 1
        piece = cb.at[b, h, pl.ds(HALF * w, HALF)]
        who = dev(x + (1 if w == 0 else NX - 1), z, c)
        go(remote(piece, piece, as_sem, fr_sem.at[FSET.index((h, n))], who))

    def take(h, e, f):
        b, n = item(e, f), ES.index(e)
        along_x = f > 0 and (h == 1 or e == 0 or (f == 3 and e in LATE))
        if along_x and f < 3:
            arrived(cb.at[b, h], hr_sem.at[XSET.index((h, n, f - 1))])
        elif along_x:
            arrived(cb.at[b, h], fr_sem.at[FSET.index((h, n))])
        elif e != 0:
            arrived(cb.at[b, h], zr_sem.at[ZSET.index((h, f, n))])
        if h == 1:
            if f == 0:
                znext(h, e, f)
                xsend(h, e)
            elif f < 3:
                xnext(h, e, f)
        else:
            if e == 0 and f == 0:
                xsend(h, e)
            if (e == 0 or e in LATE) and 0 < f < 3:
                xnext(h, e, f)
            znext(h, e, f)

    def cross(e, f):
        n = UNITS.index((e, f))
        b = item(e, f)
        go(remote(cb.at[b], cb.at[b], as_sem, cr_sem.at[n], dev(x, z, 1 - c)))

    def columns():
        for i in range(ROWS // 128):
            row = jnp.broadcast_to(slot[:, i * 128 : (i + 1) * 128], (128, 128))
            scol[i * 128 : (i + 1) * 128, :] = jnp.transpose(row).astype(jnp.int32).astype(jnp.int16)

    for l in range(3):
        arrived(tg.at[l, pl.ds(0, NY - 1)], tr_sem.at[l])
        t = tg[l].reshape(256, 512)
        for q in range(2):
            total = jnp.dot(t[:, 0:256], lvl[l, q], preferred_element_type=F32)
            if (l, q) == (0, 0):
                columns()
            for g in FILL[l][q]:
                place(g)
            arrived(part.at[l, q], br_sem.at[l, q])
            total = total + jnp.dot(t[:, 256:512], part[l, q], preferred_element_type=F32)
            if l < 2:
                lvl[l + 1, q] = total.astype(BF16)
                swap(l + 1, q).start()
            else:
                cb[leaf, q] = total.astype(BF16)
                take(q, 0, 0)
    cross(0, 0)
    nload.wait()
    for g in range(6):
        near(g)

    lanes = lax.broadcasted_iota(jnp.int32, (16, HALF), 1)
    one, zero = jnp.ones((), BF16), jnp.zeros((), BF16)

    def quad(units):
        rows, wants = [], []
        for e, f in units:
            mirror = e if e in (0, 4) else -e
            n = UNITS.index((mirror, f))
            zz = (z + 2 * NZ - d * e) % NZ
            xx = (x + SHIFT[f]) % NX
            theirs = leaf_id(xx, zz, 1 - c)
            arrived(cb.at[theirs], cr_sem.at[n])
            b0 = leaf_id(xx, zz, 0)
            wants.append((lanes + b0 * CAP).astype(jnp.int16)[None])
            for cc in range(2):
                coeff = jnp.concatenate([cb[b0 + cc, 0], cb[b0 + cc, 1]], axis=1)
                rows.append(jnp.dot(us[b0 + cc], coeff, preferred_element_type=F32).astype(BF16))
        far = jnp.concatenate(rows, axis=0)

        def back(i, carry):
            span = pl.ds(pl.multiple_of(i * 1024, 1024), 1024)
            col = scol[span, :].reshape(1024 // 16, 16, HALF)
            hot = jnp.concatenate([jnp.where(col == w, one, zero).reshape(1024, HALF) for w in wants], axis=1)
            acc[span, :] = acc[span, :] + jnp.dot(hot, far, preferred_element_type=F32)
            return carry

        lax.fori_loop(0, ROWS // 1024, back, 0)

    n = 1
    for r in range(1, 7):
        for e, f in ROUNDS[r]:
            take(0, e, f)
        for e, f in ROUNDS[r]:
            take(1, e, f)
            cross(e, f)
        n += len(ROUNDS[r])
        if r == 1:
            near(6)
            near(7)
        for lo, hi in GROUPS.get(n - 1, []):
            quad(UNITS[lo:hi])
    out_ref[...] = acc[...].astype(BF16)

    arrived(cb.at[pl.ds(0, SENT)], as_sem)
    arrived(tg.at[:, pl.ds(0, NY - 1)], ts_sem)
    arrived(lvl, bs_sem)
    arrived(sx, xs_sem)
    arrived(sv, vs_sem)
    arrived(rv.at[:, pl.ds(1, NY - 1)], ys_sem)
    arrived(ring.at[pl.ds(0, NZ - 1)], rs_sem)


def on_device(
    fields, owner, source_basis, field_basis, transfer, near_blocks, near_index, near_count
):
    vmem = pl.BlockSpec(memory_space=pltpu.VMEM)
    smem = pl.BlockSpec(memory_space=pltpu.SMEM)
    hbm = pl.BlockSpec(memory_space=pl.ANY)
    dma = pltpu.SemaphoreType.DMA
    return pl.pallas_call(
        whole_kernel,
        out_shape=pltpu.VMEM((ROWS, 256), BF16),
        in_specs=[vmem, smem, smem, hbm, hbm, hbm, hbm, hbm],
        out_specs=vmem,
        scratch_shapes=[
            pltpu.VMEM((8, 256, 256), BF16),
            pltpu.VMEM((ROWS, 256), BF16),
            pltpu.VMEM((ROWS, 256), BF16),
            pltpu.VMEM((8, 7, 256, 256), BF16),
            pltpu.VMEM((1, ROWS), F32),
            pltpu.VMEM((ROWS, HALF), jnp.int16),
            pltpu.VMEM((NZ, NG - 1, NY, Q, 256), BF16),
            pltpu.VMEM((NZ, NG - 1, Q, 256), BF16),
            pltpu.VMEM((NZ, NY, NG, Q, 256), BF16),
            pltpu.VMEM((NZ, NY, NG, Q, 256), BF16),
            pltpu.VMEM((NB, CAP, 256), BF16),
            pltpu.VMEM((NZ, 4, HALF, HALF), RING),
            pltpu.VMEM((3, 2, 256, HALF), BF16),
            pltpu.VMEM((3, 2, 256, HALF), BF16),
            pltpu.VMEM((3, NY, 64, 512), BF16),
            pltpu.VMEM((NB, 2, 256, HALF), BF16),
            pltpu.VMEM((ROWS, 256), F32),
            dma((4,)), dma(()),
            dma(()), dma((NZ,)), dma(()), dma((NZ,)), dma(()), dma((NZ,)),
            dma(()), dma((NZ - 1, 4)), dma(()), dma((3, 2)), dma(()), dma((3,)),
            dma(()), dma((len(ZSET),)), dma((len(XSET),)), dma((len(FSET),)), dma((len(UNITS),)),
        ],
        compiler_params=pltpu.CompilerParams(
            collective_id=0, has_side_effects=True, vmem_limit_bytes=58 * 1024 * 1024
        ),
    )(
        owner.reshape(1, -1), near_index, near_count, fields.reshape(8, 256, 256), source_basis, field_basis,
        transfer[0], near_blocks,
    )


def solution(mesh):
    in_specs = (
        P("leaf", "rhs"),
        P("leaf", None),
        P("leaf", None),
        P("leaf", None),
        P("leaf", None, "rhs", None),
        P("leaf", None, None, None),
        P("leaf", None),
        P("leaf"),
    )
    return jax.shard_map(
        on_device, mesh=mesh, in_specs=in_specs, out_specs=P("leaf", "rhs"), check_vma=False
    )
```
